512 devices in a mesh: ctx: 32 (over y_lo, z), fsdp: 16 (over x, y_hi, core).
Axes of the slice: x: 4, y: 4 (y_hi: 2, y_lo: 2; y = y_hi * 2 + y_lo), z: 16, core: 2. Of those that a mesh axis runs over, the one named last changes fastest.
Arguments:
- hidden_in: bfloat16 [16, 8192, 4096], P('fsdp', 'ctx'), may hold values from -40 to 40
- page_tokens: int32 [16, 16], P('fsdp'), may hold values from 1 to 1280, 8192 in all within a row
- grad_attn: bfloat16 [16, 8192, 128], P('fsdp', 'ctx'), may hold values from -6 to 6
- w_qkv: bfloat16 [4096, 384], P('fsdp'), may hold values from -1 to 1
Outputs:
- grad_hidden: bfloat16 [16, 8192, 4096], P('fsdp', 'ctx')
- grad_w_qkv: float32 [4096, 384], P('fsdp')
The draws below stay inside these ranges and needn't reach their ends.
Inputs may be any that keep to these rules, and one draw needn't show every extreme that they name: `page_tokens`: each document's page lengths sum to 8192.
All inputs are finite; a program needn't handle non-finite values.
Results may differ from the reference program's by a relative error of at most 0.039.
Values may be sent and summed in bfloat16 or wider, within the bound.
A program may use at most 128 MiB of HBM per device.

```python
import math
import jax
import jax.numpy as jnp
import numpy as np
from jax import lax

D = 4096
HD = 128
QH = 1
TOK_DEV = 256
SEQ = 8192
DOCS = 16
PAGES = 16
PAGE_MOST = 1280
N_CTX = 32


def draw_hidden_in(key, part):
    values_drawn = jax.random.truncated_normal(key, -4.0, 4.0, (DOCS, SEQ, D), jnp.float32)
    pairing = jax.random.permutation(jax.random.fold_in(key, 5), N_CTX).astype(jnp.int32)
    block_of_row = jnp.arange(SEQ, dtype=jnp.int32) // TOK_DEV
    group_of_col = jnp.arange(D, dtype=jnp.int32) // (D // N_CTX)
    heavy = pairing[block_of_row][:, None] == group_of_col[None, :]
    values_drawn = values_drawn * jnp.where(heavy, 5.0, 1.0)[None, :, :]
    return values_drawn.astype(jnp.bfloat16)


def draw_w_qkv(key, part):
    values_drawn = jax.random.truncated_normal(key, -3.0, 3.0, (D, (QH + 2) * HD), jnp.float32) * D ** (-0.5)
    return values_drawn.astype(jnp.bfloat16)


def block_scale(stream_key, extent, cuts, smallest, high):
    factor_of, own = 1.0, jax.random.fold_in(stream_key, 6)
    for dim, parts in cuts:
        heights = jnp.exp(jax.random.uniform(jax.random.fold_in(own, dim), (parts,), jnp.float32, smallest / len(cuts), high / len(cuts)))
        factor_of = factor_of * jnp.repeat(heights, extent[dim] // parts).reshape([-1 if axis == dim else 1 for axis in range(len(extent))])
    return factor_of


def length_profile(amount, total, most, skew):
    portions = [(1 << 20) // math.isqrt(standing ** skew) + 1 for standing in range(2, amount + 1)]
    spare, holding = total - most - (amount - 1), [1] * (amount - 1)
    while spare > 0:
        free = [i for i in range(amount - 1) if holding[i] < most]
        pool, remaining = sum([portions[i] for i in free]), spare
        for i in free:
            extra = min(most - holding[i], max(1, remaining * portions[i] // pool), spare)
            holding[i] = holding[i] + extra
            spare = spare - extra
    return np.array([most] + holding)


def ragged_sizes(key, amount, total, bound, slope):
    if amount == 2:
        one = jax.random.randint(key, (), max(1, total - bound), min(bound, total - 1) + 1)
        return jnp.stack([one, total - one])
    sizes = jnp.asarray(length_profile(amount, total, bound, slope), jnp.int32)
    pairs = (amount - 1) // 2
    donor, receiver = sizes[1:1 + 2 * pairs:2], sizes[2:2 + 2 * pairs:2]
    room = jnp.minimum(donor - 1, bound - receiver)
    moved = jax.random.randint(jax.random.fold_in(key, 1), (pairs,), 0, 1 << 20) % (room + 1)
    sizes = sizes.at[1:1 + 2 * pairs:2].set(donor - moved).at[2:2 + 2 * pairs:2].set(receiver + moved)
    return sizes[jax.random.permutation(jax.random.fold_in(key, 2), amount)]


def noise(own_key, extent, deviation, bound, cuts=(), kind=jnp.bfloat16):
    drawn = jax.random.normal(own_key, extent, jnp.float32) * deviation
    if len(cuts) > 0:
        drawn = block_scale(own_key, extent, cuts, -0.22, 0.18) * drawn
    return jnp.clip(drawn, min=-bound, max=bound).astype(kind)


def setup_inputs(seed: int = 0) -> dict:
    streams_of = jax.random.split(jax.random.key(seed), 5)
    hidden_in = draw_hidden_in(jax.random.fold_in(streams_of[4], 71), 0)
    page_tokens = jax.vmap(lambda own: ragged_sizes(own, PAGES, SEQ, PAGE_MOST, 1))(jax.random.split(streams_of[1], DOCS)).reshape((DOCS, PAGES)).astype(jnp.int32)
    grad_attn = noise(streams_of[2], (DOCS, SEQ, QH * HD), 1.0, 6.0, ((0, 16), (1, 32)))
    w_qkv = draw_w_qkv(jax.random.fold_in(streams_of[4], 71), 0)
    return dict(hidden_in=hidden_in, page_tokens=page_tokens, grad_attn=grad_attn, w_qkv=w_qkv)


def page_limits(page_row, positions, total_len):
    page_ends = jnp.cumsum(page_row).astype(jnp.int32)
    return jnp.min(jnp.where(page_ends[None, :] > positions[:, None], page_ends[None, :], total_len), axis=1)


def reference(hidden_in, page_tokens, grad_attn, w_qkv):
    score_scale = HD ** -0.5

    def one_doc(doc_args):
        inputs_doc, page_row, grad_out = doc_args
        projected = jnp.dot(inputs_doc, w_qkv, preferred_element_type=jnp.float32).astype(jnp.bfloat16)
        queries = projected[:, :HD]
        keys_all = projected[:, HD:2 * HD]
        values_all = projected[:, 2 * HD:]
        key_pos = jnp.arange(SEQ, dtype=jnp.int32)
        limits = page_limits(page_row, key_pos, SEQ)
        visible = key_pos[None, :] < limits[:, None]
        scores = jnp.where(visible, jnp.dot(queries, keys_all.T, preferred_element_type=jnp.float32) * score_scale, -1e30)
        row_max = jnp.max(scores, axis=1, keepdims=True)
        log_total = row_max[:, 0] + jnp.log(jnp.sum(jnp.exp(scores - row_max), axis=1))
        probs_full = jnp.exp(scores - log_total[:, None])
        probs_half = probs_full.astype(jnp.bfloat16)
        attended = jnp.dot(probs_half, values_all, preferred_element_type=jnp.float32)
        out_dot = jnp.sum(grad_out.astype(jnp.float32) * attended, axis=1)
        dprob = jnp.dot(grad_out, values_all.T, preferred_element_type=jnp.float32)
        dscore = (probs_full * (dprob - out_dot[:, None]) * score_scale).astype(jnp.bfloat16)
        query_grad = jnp.dot(dscore, keys_all, preferred_element_type=jnp.float32)
        key_grad = jnp.dot(dscore.T, queries, preferred_element_type=jnp.float32)
        value_grad = jnp.dot(probs_half.T, grad_out, preferred_element_type=jnp.float32)
        grad_qkv = jnp.concatenate([query_grad, key_grad, value_grad], axis=1).astype(jnp.bfloat16)
        grad_inputs = jnp.dot(grad_qkv, w_qkv.T, preferred_element_type=jnp.float32).astype(jnp.bfloat16)
        blocks_in = inputs_doc.reshape(N_CTX, TOK_DEV, D)
        blocks_grad = grad_qkv.reshape(N_CTX, TOK_DEV, (QH + 2) * HD)

        def block_step(running, block_pair):
            block_term = jnp.dot(block_pair[0].T, block_pair[1], preferred_element_type=jnp.float32).astype(jnp.bfloat16)
            return running + lax.optimization_barrier(block_term).astype(jnp.float32), None

        weight_sum, _ = lax.scan(block_step, jnp.zeros((D, (QH + 2) * HD), jnp.float32), (blocks_in, blocks_grad))
        return grad_inputs, weight_sum

    grad_hidden, weight_terms = lax.map(one_doc, (hidden_in, page_tokens, grad_attn))
    return grad_hidden, jnp.sum(weight_terms, axis=0)
```

```python
import functools

import jax
import jax.numpy as jnp
from jax import lax
from jax.experimental import pallas as pl
from jax.experimental.pallas import tpu as pltpu
from jax.sharding import PartitionSpec as P

MESH = pl.DeviceIdType.MESH
F32, BF16 = jnp.float32, jnp.bfloat16
NX, NYH, NC, NYL, NZ = 4, 2, 2, 2, 16
TOK, HD, D = 256, 128, 4096
QKV = 3 * HD
ROWS = D // (NX * NYH * NC)
NEG = -1e30
SCALE = HD ** -0.5
REACH = 5
HALF = TOK // 2
PAGES = 16


def fsdp_id(x, yh, core):
    return (x * NYH + yh) * NC + core


def ctx_id(yl, z):
    return yl * NZ + z


def place():
    ctx, f = lax.axis_index("ctx"), lax.axis_index("fsdp")
    return ctx // NZ, ctx % NZ, f // (NYH * NC), (f // NC) % NYH, f % NC


def rcopy(src, dst, send, recv, dev):
    return pltpu.make_async_remote_copy(
        src_ref=src, dst_ref=dst, send_sem=send, recv_sem=recv, device_id=dev, device_id_type=MESH
    )


def greet(peers):
    barrier = pltpu.get_barrier_semaphore()
    for dev in peers:
        pl.semaphore_signal(barrier, inc=1, device_id=dev, device_id_type=MESH)
    pl.semaphore_wait(barrier, len(peers))


def nt(a, b):
    return lax.dot_general(a, b, (((1,), (1,)), ((), ())), preferred_element_type=F32)


def tn(a, b):
    return lax.dot_general(a, b, (((0,), (0,)), ((), ())), preferred_element_type=F32)


def nn(a, b):
    return jnp.dot(a, b, preferred_element_type=F32)


def neighbours():
    yl, z, x, yh, core = place()
    ctx, f = ctx_id(yl, z), fsdp_id(x, yh, core)
    left, right = (x + NX - 1) % NX, (x + 1) % NX
    dev_l, dev_r = (ctx, fsdp_id(left, yh, core)), (ctx, fsdp_id(right, yh, core))
    dev_y = (ctx_id(1 - yl, z), fsdp_id(x, 1 - yh, core))
    dev_s = (ctx, fsdp_id(x, yh, 1 - core))
    return dev_l, dev_r, dev_y, dev_s


def gather_kernel(
    hid_hbm, w_hbm, do_hbm, wall_out, proj_out, doall, pdo,
    hid, wall, wsend, wrecv, dsend, drecv, loc,
):
    yl, z, x, yh, core = place()
    ctx, f = ctx_id(yl, z), fsdp_id(x, yh, core)
    left, right, far = (x + NX - 1) % NX, (x + 1) % NX, (x + 2) % NX
    dev_l, dev_r, dev_y, dev_s = neighbours()
    dev_p = (ctx_id(1 - yl, z), f)
    dev_zl, dev_zr = (ctx_id(yl, (z + NZ - 1) % NZ), f), (ctx_id(yl, (z + 1) % NZ), f)
    greet([dev_l, dev_r, dev_y, dev_s, dev_p, dev_zl, dev_zr])

    hid_copy = pltpu.make_async_copy(hid_hbm, hid, loc.at[0])
    own_copy = pltpu.make_async_copy(w_hbm, wall.at[f], loc.at[1])
    do_copy = pltpu.make_async_copy(do_hbm, doall.at[z], loc.at[2])
    sent = []

    def send(src, dst, slot, dev):
        copy = rcopy(src, dst, wsend.at[len(sent)], wrecv.at[slot], dev)
        copy.start()
        sent.append(copy)

    def arrived(ref, slot):
        rcopy(ref, ref, wsend.at[0], wrecv.at[slot], dev_s).wait_recv()

    lo, hi = pl.ds(0, HALF), pl.ds(HALF, HALF)
    for slot, dev in ((1, dev_r), (2, dev_l), (0, dev_y), (9, dev_s)):
        send(w_hbm, wall.at[f], slot, dev)
    own_copy.start()
    do_copy.start()
    hid_copy.start()
    dsent = []

    def dsendto(src, dst, slot, dev):
        copy = rcopy(src, dst, dsend.at[len(dsent)], drecv.at[slot], dev)
        copy.start()
        dsent.append(copy)

    dsendto(do_hbm, doall.at[z], 1, dev_zr)
    dsendto(do_hbm, doall.at[z], 9, dev_zl)
    dsendto(do_hbm, pdo, 0, dev_p)

    def do_step(d):
        zl, zr = (z + NZ - d) % NZ, (z + d) % NZ
        from_l, from_r = doall.at[zl], doall.at[zr]
        if d == NZ // 2:
            from_l, from_r = doall.at[zl, lo], doall.at[zr, hi]
        rcopy(from_l, from_l, dsend.at[0], drecv.at[d], dev_p).wait_recv()
        if d < NZ // 2:
            on = doall.at[zl, lo] if d == NZ // 2 - 1 else from_l
            dsendto(on, on, d + 1, dev_zr)
        rcopy(from_r, from_r, dsend.at[0], drecv.at[8 + d], dev_p).wait_recv()
        if d < NZ // 2:
            on = doall.at[zr, hi] if d == NZ // 2 - 1 else from_r
            dsendto(on, on, 9 + d, dev_zl)

    def own(xx, yy):
        return fsdp_id(xx, yy, core)

    def sib(xx, yy):
        return fsdp_id(xx, yy, 1 - core)

    yc = 1 - yh
    c = wall.at[own(x, yc)]
    arrived(c, 0)
    send(c, c, 3, dev_r)
    send(c, c, 4, dev_l)
    send(c, c, 10, dev_s)
    ol, orr = wall.at[own(left, yh)], wall.at[own(right, yh)]
    arrived(ol, 1)
    on = wall.at[own(left, yh), lo]
    send(on, on, 5, dev_r)
    send(ol, ol, 11, dev_s)
    arrived(orr, 2)
    on = wall.at[own(right, yh), hi]
    send(on, on, 6, dev_l)
    send(orr, orr, 12, dev_s)
    do_step(1)
    fa, fb = wall.at[own(far, yh), lo], wall.at[own(far, yh), hi]
    arrived(fa, 5)
    send(fa, fa, 7, dev_y)
    send(fa, fa, 15, dev_s)
    arrived(fb, 6)
    send(fb, fb, 8, dev_y)
    send(fb, fb, 16, dev_s)
    do_step(2)
    cl, cr = wall.at[own(left, yc)], wall.at[own(right, yc)]
    arrived(cl, 3)
    send(cl, cl, 13, dev_s)
    arrived(cr, 4)
    send(cr, cr, 14, dev_s)
    do_step(3)
    ca, cb = wall.at[own(far, yc), lo], wall.at[own(far, yc), hi]
    arrived(ca, 7)
    send(ca, ca, 17, dev_s)
    arrived(cb, 8)
    send(cb, cb, 18, dev_s)
    do_step(4)
    for slot, ref in (
        (9, wall.at[sib(x, yh)]), (10, wall.at[sib(x, yc)]), (11, wall.at[sib(left, yh)]),
        (12, wall.at[sib(right, yh)]), (13, wall.at[sib(left, yc)]), (14, wall.at[sib(right, yc)]),
        (15, wall.at[sib(far, yh), lo]), (16, wall.at[sib(far, yh), hi]),
        (17, wall.at[sib(far, yc), lo]), (18, wall.at[sib(far, yc), hi]),
    ):
        arrived(ref, slot)
    own_copy.wait()
    wall_copy = pltpu.make_async_copy(wall, wall_out, loc.at[1])
    wall_copy.start()
    hid_copy.wait()
    total = jnp.zeros((TOK, QKV), F32)
    for s in range(NX * NYH * NC):
        if s in (0, 5, 10):
            do_step(5 + s // 5)
        total += nn(hid[:, s * ROWS : (s + 1) * ROWS], wall[s])
    proj_out[...] = total.astype(BF16)
    do_step(8)
    rcopy(pdo, pdo, dsend.at[0], drecv.at[0], dev_p).wait_recv()
    for copy in sent + dsent:
        copy.wait_send()
    do_copy.wait()
    wall_copy.wait()


def gather_weights(hidden, w, grad_out):
    n = NX * NYH * NC
    any_spec = pl.BlockSpec(memory_space=pl.ANY)
    vmem = pl.BlockSpec(memory_space=pltpu.VMEM)
    return pl.pallas_call(
        gather_kernel,
        out_shape=(
            jax.ShapeDtypeStruct((n, ROWS, QKV), BF16),
            jax.ShapeDtypeStruct((TOK, QKV), BF16),
            jax.ShapeDtypeStruct((NZ, TOK, HD), BF16),
            jax.ShapeDtypeStruct((TOK, HD), BF16),
        ),
        in_specs=[any_spec] * 3,
        out_specs=(any_spec, vmem, vmem, vmem),
        scratch_shapes=[
            pltpu.VMEM((TOK, D), BF16),
            pltpu.VMEM((n, ROWS, QKV), BF16),
            pltpu.SemaphoreType.DMA((19,)),
            pltpu.SemaphoreType.DMA((19,)),
            pltpu.SemaphoreType.DMA((17,)),
            pltpu.SemaphoreType.DMA((17,)),
            pltpu.SemaphoreType.DMA((3,)),
        ],
        compiler_params=pltpu.CompilerParams(
            collective_id=0, has_side_effects=True, vmem_limit_bytes=24 << 20
        ),
        name="gather_weights",
    )(hidden, w, grad_out)


def attend_kernel(
    pages, proj, doall, pdo, grad_qkv,
    qkv, pqkv, q2, do2, lim_q, lim_col, s_keep, dp_keep, mlu, mlu_in, stats, dqt, dkv, out_x, in_x, out_kv, in_kv,
    zsend, zrecv, psend, precv, ssend, srecv,
):
    yl, z, x, yh, core = place()
    f = fsdp_id(x, yh, core)
    dev_p = (ctx_id(1 - yl, z), f)

    def at_z(d):
        return (ctx_id(yl, (z + d) % NZ), f)

    dev_zl, dev_zr = at_z(NZ - 1), at_z(1)
    greet([dev_p] + [at_z(d) for d in range(1, NZ)])
    lo, hi = pl.ds(0, HALF), pl.ds(HALF, HALF)

    first = [
        rcopy(proj, qkv.at[z], zsend.at[0, 0], zrecv.at[0, 1], dev_zr),
        rcopy(proj, qkv.at[z], zsend.at[1, 0], zrecv.at[1, 1], dev_zl),
        rcopy(proj, pqkv, psend.at[0], precv.at[0], dev_p),
    ]
    for copy in first:
        copy.start()
    qkv[z] = proj[...]

    ends = []
    total = 0
    for page in range(PAGES):
        total = total + pages[0, page]
        ends.append(total)

    def limits(pos):
        out = jnp.full(pos.shape, NYL * NZ * TOK, jnp.int32)
        for end in ends:
            out = jnp.minimum(out, jnp.where(pos < end, end, NYL * NZ * TOK))
        return out

    lane = lax.broadcasted_iota(jnp.int32, (1, TOK), 1)
    lim_q[:, :TOK] = limits(ctx_id(yl, z) * TOK + lane)
    lim_q[:, TOK:] = limits(ctx_id(1 - yl, z) * TOK + lane)

    @pl.loop(0, NZ)
    def _(j):
        lim_col[j] = limits(ctx_id(yl, j) * TOK + lane)

    q2[:TOK] = proj[:, :HD]
    do2[:TOK] = doall[z]
    do2[TOK:] = pdo[...]
    mlu[0:1] = jnp.full((1, 2 * TOK), NEG, F32)
    mlu[1:8] = jnp.zeros((7, 2 * TOK), F32)
    first[2].wait_recv()
    q2[TOK:] = pqkv[:, :HD]

    key_row = lax.broadcasted_iota(jnp.int32, (TOK, 1), 0)

    def score_block(j):
        s = nt(qkv[j, :, HD : 2 * HD], q2[...]) * SCALE
        dp = nt(qkv[j, :, 2 * HD :], do2[...])
        s = jnp.where(ctx_id(yl, j) * TOK + key_row < lim_q[...], s, NEG)
        s_keep[j] = s
        dp_keep[j] = dp
        m = mlu[0:1]
        m_new = jnp.maximum(m, jnp.max(s, axis=0, keepdims=True))
        p = jnp.exp(s - m_new)
        a = jnp.exp(m - m_new)
        mlu[0:1] = m_new
        mlu[1:2] = mlu[1:2] * a + jnp.sum(p, axis=0, keepdims=True)
        mlu[2:3] = mlu[2:3] * a + jnp.sum(p * dp, axis=0, keepdims=True)

    last_q = ctx_id(1, z)

    def score(j):
        @pl.when(ctx_id(yl, j) <= last_q + REACH)
        def _():
            score_block(j)

    score(z)

    def passed(d):
        zl, zr = (z + NZ - d) % NZ, (z + d) % NZ
        rcopy(qkv.at[zl], qkv.at[zl], zsend.at[0, d], zrecv.at[0, d], dev_zr).wait_recv()
        return zl, zr

    @pl.loop(1, NZ // 2 - 1)
    def _(d):
        zl, zr = passed(d)
        rcopy(qkv.at[zl], qkv.at[zl], zsend.at[0, d], zrecv.at[0, d + 1], dev_zr).start()
        rcopy(qkv.at[zr], qkv.at[zr], zsend.at[1, d], zrecv.at[1, d], dev_zl).wait_recv()
        rcopy(qkv.at[zr], qkv.at[zr], zsend.at[1, d], zrecv.at[1, d + 1], dev_zl).start()

        @pl.loop(0, 2)
        def _(side):
            score((z + NZ - d + 2 * d * side) % NZ)

    d = NZ // 2 - 1
    zl, zr = passed(d)
    on = qkv.at[zl, lo]
    tail_r = rcopy(on, on, zsend.at[0, d], zrecv.at[0, d + 1], dev_zr)
    tail_r.start()
    rcopy(qkv.at[zr], qkv.at[zr], zsend.at[1, d], zrecv.at[1, d], dev_zl).wait_recv()
    on = qkv.at[zr, hi]
    tail_l = rcopy(on, on, zsend.at[1, d], zrecv.at[1, d + 1], dev_zl)
    tail_l.start()
    score(zl)
    score(zr)
    opp = (z + NZ // 2) % NZ
    rcopy(qkv.at[opp, lo], qkv.at[opp, lo], zsend.at[0, 0], zrecv.at[0, d + 1], dev_zr).wait_recv()
    rcopy(qkv.at[opp, hi], qkv.at[opp, hi], zsend.at[1, 0], zrecv.at[1, d + 1], dev_zl).wait_recv()
    score(opp)

    trade = rcopy(mlu, mlu_in, psend.at[1], precv.at[1], dev_p)
    trade.start()
    trade.wait_recv()

    def merge(mine, theirs):
        m1, m2 = mlu[0:1, mine], mlu_in[0:1, theirs]
        m = jnp.maximum(m1, m2)
        a1, a2 = jnp.exp(m1 - m), jnp.exp(m2 - m)
        l = mlu[1:2, mine] * a1 + mlu_in[1:2, theirs] * a2
        u = mlu[2:3, mine] * a1 + mlu_in[2:3, theirs] * a2
        return m + jnp.log(l), u / l

    own_q, par_q = slice(0, TOK), slice(TOK, 2 * TOK)
    lse_own, dot_own = merge(own_q, par_q)
    lse_par, dot_par = merge(par_q, own_q)
    stats[z, 0:1] = lse_own
    stats[z, 1:2] = dot_own
    stats[z, 2:8] = jnp.zeros((6, TOK), F32)

    @pl.loop(1, NZ)
    def _(d):
        rcopy(stats.at[z], stats.at[z], ssend.at[d], srecv.at[d], at_z(d)).start()

    trade.wait_send()
    mlu[0:1] = jnp.concatenate([lse_own, lse_par], axis=1)
    mlu[1:2] = jnp.concatenate([dot_own, dot_par], axis=1)
    dqt[...] = jnp.zeros((HD, 2 * TOK), F32)

    @pl.loop(0, NZ)
    def _(j):
        @pl.when(ctx_id(yl, j) <= last_q + REACH)
        def _():
            p = jnp.exp(s_keep[j] - mlu[0:1])
            ds = (p * (dp_keep[j] - mlu[1:2]) * SCALE).astype(BF16)
            dqt[...] += tn(qkv[j, :, HD : 2 * HD], ds)

    out_x[...] = dqt[:, TOK:].astype(BF16)
    dq_copy = rcopy(out_x, in_x, psend.at[2], precv.at[2], dev_p)
    dq_copy.start()

    def key_block(src, k_block, j):
        s = nt(src[:, HD : 2 * HD], qkv[j, :, :HD]) * SCALE
        dp = nt(src[:, 2 * HD :], doall[j])
        s = jnp.where(k_block * TOK + key_row < lim_col[j], s, NEG)
        p = jnp.exp(s - stats[j, 0:1])
        ds = (p * (dp - stats[j, 1:2]) * SCALE).astype(BF16)
        dkv[:, :HD] += nn(ds, qkv[j, :, :HD])
        dkv[:, HD:] += nn(p.astype(BF16), doall[j])

    def keys(src, k_block, wait):
        dkv[...] = jnp.zeros((TOK, 2 * HD), F32)

        @pl.loop(0, NZ)
        def _(d):
            j = (z + NZ - d) % NZ
            if wait:
                @pl.when(d > 0)
                def _():
                    rcopy(stats.at[j], stats.at[j], ssend.at[d], srecv.at[d], dev_p).wait_recv()

            @pl.when(k_block <= ctx_id(yl, j) + REACH)
            def _():
                key_block(src, k_block, j)

    keys(pqkv, ctx_id(1 - yl, z), True)
    out_kv[...] = dkv[...].astype(BF16)
    kv_copy = rcopy(out_kv, in_kv, psend.at[3], precv.at[3], dev_p)
    kv_copy.start()
    keys(proj, ctx_id(yl, z), False)
    dq_copy.wait_recv()
    grad_qkv[:, :HD] = (dqt[:, :TOK] + in_x[...].astype(F32)).T.astype(BF16)
    kv_copy.wait_recv()
    grad_qkv[:, HD:] = (dkv[...] + in_kv[...].astype(F32)).astype(BF16)

    for copy in first:
        copy.wait_send()

    @pl.loop(1, NZ // 2 - 1)
    def _(d):
        rcopy(proj, proj, zsend.at[0, d], zrecv.at[0, d], dev_zr).wait_send()
        rcopy(proj, proj, zsend.at[1, d], zrecv.at[1, d], dev_zl).wait_send()

    tail_r.wait_send()
    tail_l.wait_send()
    dq_copy.wait_send()
    kv_copy.wait_send()

    @pl.loop(1, NZ)
    def _(d):
        rcopy(stats.at[z], stats.at[z], ssend.at[d], srecv.at[d], dev_p).wait_send()


def attend(pages, proj, doall, pdo):
    vmem = pl.BlockSpec(memory_space=pltpu.VMEM)
    dma = pltpu.SemaphoreType.DMA
    return pl.pallas_call(
        attend_kernel,
        out_shape=jax.ShapeDtypeStruct((TOK, QKV), BF16),
        in_specs=[pl.BlockSpec(memory_space=pltpu.SMEM), vmem, vmem, vmem],
        out_specs=vmem,
        scratch_shapes=[
            pltpu.VMEM((NZ, TOK, QKV), BF16),
            pltpu.VMEM((TOK, QKV), BF16),
            pltpu.VMEM((2 * TOK, HD), BF16),
            pltpu.VMEM((2 * TOK, HD), BF16),
            pltpu.VMEM((1, 2 * TOK), jnp.int32),
            pltpu.VMEM((NZ, 1, TOK), jnp.int32),
            pltpu.VMEM((NZ, TOK, 2 * TOK), F32),
            pltpu.VMEM((NZ, TOK, 2 * TOK), F32),
            pltpu.VMEM((8, 2 * TOK), F32),
            pltpu.VMEM((8, 2 * TOK), F32),
            pltpu.VMEM((NZ, 8, TOK), F32),
            pltpu.VMEM((HD, 2 * TOK), F32),
            pltpu.VMEM((TOK, 2 * HD), F32),
            pltpu.VMEM((HD, TOK), BF16),
            pltpu.VMEM((HD, TOK), BF16),
            pltpu.VMEM((TOK, 2 * HD), BF16),
            pltpu.VMEM((TOK, 2 * HD), BF16),
            dma((2, NZ // 2)),
            dma((2, NZ // 2 + 1)),
            dma((4,)),
            dma((4,)),
            dma((NZ,)),
            dma((NZ,)),
        ],
        compiler_params=pltpu.CompilerParams(
            collective_id=1, has_side_effects=True, vmem_limit_bytes=40 << 20
        ),
        name="attend",
    )(pages, proj, doall, pdo)


PATCH = 8
SLICE = ROWS // PATCH


def reduce_kernel(
    hid_hbm, gq, gw_out,
    hid, term, sib, sib_in, got, gotb, relay, total, part, part_in, mid, mid_in, fin, loc, csend, crecv, nsend, nrecv, asend, arecv,
):
    yl, z, x, yh, core = place()
    ctx, f = ctx_id(yl, z), fsdp_id(x, yh, core)
    dev_l, dev_r, dev_y, dev_s = neighbours()
    zl, zh = z % 4, z // 4

    def patch_dev(i):
        return (ctx_id(i // 4, zh * 4 + i % 4), f)

    me = yl * 4 + zl
    peers = [(me + i) % PATCH for i in range(1, PATCH)]
    far_z = [(ctx_id(yl, (z + 4 * i) % NZ), f) for i in range(1, 4)]
    hid_copy = pltpu.make_async_copy(hid_hbm, hid, loc.at[0])
    hid_copy.start()
    greet([dev_l, dev_r, dev_y, dev_s] + [patch_dev(i) for i in peers] + far_z)
    hid_copy.wait()

    n8 = NX * NYH
    lo, hi = pl.ds(0, HALF), pl.ds(HALF, HALF)

    def block(s):
        return tn(hid[:, pl.ds(pl.multiple_of(s * ROWS, ROWS), ROWS)], gq[...])

    @pl.loop(0, n8)
    def _(i):
        sib[i] = block(2 * i + 1 - core).astype(BF16)
        rcopy(sib.at[i], sib_in.at[i], csend.at[i], crecv.at[i], dev_s).start()

    @pl.loop(0, n8)
    def _(i):
        mine = block(2 * i + core)
        rcopy(sib_in.at[i], sib_in.at[i], csend.at[i], crecv.at[i], dev_s).wait_recv()
        term[i] = (mine + sib_in[i].astype(F32)).astype(BF16)

    left, right, far = (x + NX - 1) % NX, (x + 1) % NX, (x + 2) % NX
    yc = 1 - yh

    def at(xx, yy):
        return xx * NYH + yy

    sent = []

    def send(src, dst, slot, dev):
        copy = rcopy(src, dst, nsend.at[len(sent)], nrecv.at[slot], dev)
        copy.start()
        sent.append(copy)

    def arrived(ref, slot):
        rcopy(ref, ref, nsend.at[0], nrecv.at[slot], dev_s).wait_recv()

    send(term.at[at(far, yc)], got.at[0], 0, dev_y)
    send(term.at[at(left, yc)], got.at[2], 2, dev_l)
    send(term.at[at(right, yc)], got.at[1], 1, dev_r)
    arrived(got.at[0], 0)
    relay[0] = (term[at(far, yh)].astype(F32) + got[0].astype(F32)).astype(BF16)
    send(relay.at[0, lo], gotb.at[0], 6, dev_r)
    send(relay.at[0, hi], gotb.at[1], 7, dev_l)
    arrived(got.at[1], 1)
    arrived(got.at[2], 2)
    relay[1] = (term[at(x, yc)].astype(F32) + got[1].astype(F32) + got[2].astype(F32)).astype(BF16)
    send(relay.at[1], got.at[5], 5, dev_y)
    arrived(gotb.at[0], 6)
    relay[2, :HALF] = (term[at(right, yh), :HALF].astype(F32) + gotb[0].astype(F32)).astype(BF16)
    relay[2, HALF:] = term[at(right, yh), HALF:]
    send(relay.at[2], got.at[3], 3, dev_r)
    arrived(gotb.at[1], 7)
    relay[3, HALF:] = (term[at(left, yh), HALF:].astype(F32) + gotb[1].astype(F32)).astype(BF16)
    relay[3, :HALF] = term[at(left, yh), :HALF]
    send(relay.at[3], got.at[4], 4, dev_l)
    arrived(got.at[5], 5)
    arrived(got.at[3], 3)
    arrived(got.at[4], 4)
    total[...] = (
        term[at(x, yh)].astype(F32) + got[3].astype(F32) + got[4].astype(F32) + got[5].astype(F32)
    )
    part[...] = total[...].astype(BF16).reshape(PATCH, SLICE, QKV)

    for i in range(1, PATCH):
        to = (me + i) % PATCH
        copy = rcopy(part.at[to], part_in.at[i], asend.at[i], arecv.at[i], patch_dev(to))
        copy.start()
        sent.append(copy)
    acc = total[pl.ds(pl.multiple_of(me * SLICE, SLICE), SLICE), :]
    for i in range(1, PATCH):
        rcopy(part_in.at[i], part_in.at[i], asend.at[i], arecv.at[i], dev_s).wait_recv()
        acc += part_in[i].astype(F32)
    mid[...] = acc.astype(BF16)
    for i in range(1, 4):
        copy = rcopy(mid, mid_in.at[i], asend.at[7 + i], arecv.at[7 + i], far_z[i - 1])
        copy.start()
        sent.append(copy)
    for i in range(1, 4):
        rcopy(mid_in.at[i], mid_in.at[i], asend.at[7 + i], arecv.at[7 + i], dev_s).wait_recv()
    mid_in[0] = mid[...]
    acc = jnp.zeros((SLICE, QKV), F32)
    for h in range(4):
        acc += mid_in[(zh - h + 4) % 4].astype(F32)
    fin[me] = acc.astype(BF16)
    for i in range(1, PATCH):
        to = (me + i) % PATCH
        copy = rcopy(fin.at[me], fin.at[me], asend.at[10 + i], arecv.at[10 + i], patch_dev(to))
        copy.start()
        sent.append(copy)
    for i in range(1, PATCH):
        src = fin.at[(me + PATCH - i) % PATCH]
        rcopy(src, src, asend.at[10 + i], arecv.at[10 + i], dev_s).wait_recv()
    gw_out[...] = fin[...].reshape(ROWS, QKV).astype(F32)
    for copy in sent:
        copy.wait_send()

    @pl.loop(0, n8)
    def _(i):
        rcopy(sib.at[i], sib_in.at[i], csend.at[i], crecv.at[i], dev_s).wait_send()


def reduce_weights(hidden, gq):
    n8 = NX * NYH
    vmem = pl.BlockSpec(memory_space=pltpu.VMEM)
    dma = pltpu.SemaphoreType.DMA
    return pl.pallas_call(
        reduce_kernel,
        out_shape=jax.ShapeDtypeStruct((ROWS, QKV), F32),
        in_specs=[pl.BlockSpec(memory_space=pl.ANY), vmem],
        out_specs=vmem,
        scratch_shapes=[
            pltpu.VMEM((TOK, D), BF16),
            pltpu.VMEM((n8, ROWS, QKV), BF16),
            pltpu.VMEM((n8, ROWS, QKV), BF16),
            pltpu.VMEM((n8, ROWS, QKV), BF16),
            pltpu.VMEM((6, ROWS, QKV), BF16),
            pltpu.VMEM((2, HALF, QKV), BF16),
            pltpu.VMEM((4, ROWS, QKV), BF16),
            pltpu.VMEM((ROWS, QKV), F32),
            pltpu.VMEM((PATCH, SLICE, QKV), BF16),
            pltpu.VMEM((PATCH, SLICE, QKV), BF16),
            pltpu.VMEM((SLICE, QKV), BF16),
            pltpu.VMEM((4, SLICE, QKV), BF16),
            pltpu.VMEM((PATCH, SLICE, QKV), BF16),
            dma((1,)),
            dma((n8,)),
            dma((n8,)),
            dma((8,)),
            dma((8,)),
            dma((18,)),
            dma((18,)),
        ],
        compiler_params=pltpu.CompilerParams(
            collective_id=2, has_side_effects=True, vmem_limit_bytes=32 << 20
        ),
        name="reduce_weights",
    )(hidden, gq)


def local(hidden_in, page_tokens, grad_attn, w_qkv):
    hidden = hidden_in[0]
    wall, proj, doall, pdo = gather_weights(hidden, w_qkv, grad_attn[0])
    gq = attend(page_tokens, proj, doall, pdo)
    grad_w = reduce_weights(hidden, gq)
    grad_hidden = nt(gq, wall.reshape(D, QKV)).astype(BF16)[None]
    return grad_hidden, grad_w


def solution(mesh):
    in_specs = (P("fsdp", "ctx", None), P("fsdp", None), P("fsdp", "ctx", None), P("fsdp", None))
    out_specs = (P("fsdp", "ctx", None), P("fsdp", None))
    return jax.shard_map(local, mesh=mesh, in_specs=in_specs, out_specs=out_specs, check_vma=False)
```

```python
import functools

import jax
import jax.numpy as jnp
from jax import lax
from jax.experimental import pallas as pl
from jax.experimental.pallas import tpu as pltpu
from jax.sharding import PartitionSpec as P

MESH = pl.DeviceIdType.MESH
F32, BF16 = jnp.float32, jnp.bfloat16
NX, NYH, NC, NYL, NZ = 4, 2, 2, 2, 16
TOK, HD, D = 256, 128, 4096
QKV = 3 * HD
ROWS = D // (NX * NYH * NC)
NEG = -1e30
SCALE = HD ** -0.5
REACH = 5
HALF = TOK // 2
PAGES = 16
LAG = 3


def fsdp_id(x, yh, core):
    return (x * NYH + yh) * NC + core


def ctx_id(yl, z):
    return yl * NZ + z


def place():
    ctx, f = lax.axis_index("ctx"), lax.axis_index("fsdp")
    return ctx // NZ, ctx % NZ, f // (NYH * NC), (f // NC) % NYH, f % NC


def rcopy(src, dst, send, recv, dev):
    return pltpu.make_async_remote_copy(
        src_ref=src, dst_ref=dst, send_sem=send, recv_sem=recv, device_id=dev, device_id_type=MESH
    )


def greet(peers):
    barrier = pltpu.get_barrier_semaphore()
    for dev in peers:
        pl.semaphore_signal(barrier, inc=1, device_id=dev, device_id_type=MESH)
    pl.semaphore_wait(barrier, len(peers))


def nt(a, b):
    return lax.dot_general(a, b, (((1,), (1,)), ((), ())), preferred_element_type=F32)


def tn(a, b):
    return lax.dot_general(a, b, (((0,), (0,)), ((), ())), preferred_element_type=F32)


def nn(a, b):
    return jnp.dot(a, b, preferred_element_type=F32)


def neighbours():
    yl, z, x, yh, core = place()
    ctx, f = ctx_id(yl, z), fsdp_id(x, yh, core)
    left, right = (x + NX - 1) % NX, (x + 1) % NX
    dev_l, dev_r = (ctx, fsdp_id(left, yh, core)), (ctx, fsdp_id(right, yh, core))
    dev_y = (ctx_id(1 - yl, z), fsdp_id(x, 1 - yh, core))
    dev_s = (ctx, fsdp_id(x, yh, 1 - core))
    return dev_l, dev_r, dev_y, dev_s


def front_kernel(
    pages, hid_hbm, w_hbm, do_hbm, wall_out, grad_qkv,
    hid, wall, acc, proj, pqkv, kall, vall, qall, doall, pdo, q2, do2, lim_q, lim_col, s_keep, dp_keep, mlu, mlu_in,
    stats, dqt, dkv, out_x, in_x, out_kv, in_kv, wsend, wrecv, zsend, zrecv, psend, precv, ssend, srecv, loc,
):
    yl, z, x, yh, core = place()
    ctx, f = ctx_id(yl, z), fsdp_id(x, yh, core)
    left, right, far = (x + NX - 1) % NX, (x + 1) % NX, (x + 2) % NX
    dev_l, dev_r, dev_y, dev_s = neighbours()
    dev_p = (ctx_id(1 - yl, z), f)

    def at_z(d):
        return (ctx_id(yl, (z + d) % NZ), f)

    dev_zl, dev_zr = at_z(NZ - 1), at_z(1)
    greet([dev_l, dev_r, dev_y, dev_s, dev_p, dev_zl, dev_zr])

    sent = []

    def send(src, dst, slot, dev):
        copy = rcopy(src, dst, wsend.at[len(sent)], wrecv.at[slot], dev)
        copy.start()
        sent.append(copy)

    def arrived(ref, slot):
        rcopy(ref, ref, wsend.at[0], wrecv.at[slot], dev_s).wait_recv()

    rings = ((kall, 8, 7), (vall, 7, 8), (qall, 8, 7), (doall, 7, 8))

    def ring_start(u, src):
        buf = rings[u][0]
        rcopy(src, buf.at[z], zsend.at[u, 0, 0], zrecv.at[u, 0, 1], dev_zr).start()
        rcopy(src, buf.at[z], zsend.at[u, 1, 0], zrecv.at[u, 1, 1], dev_zl).start()

    def serve(u, d):
        buf, reach_r, reach_l = rings[u]
        for side, reach, dev, j in (
            (0, reach_r, dev_zr, (z + NZ - d) % NZ), (1, reach_l, dev_zl, (z + d) % NZ)
        ):
            @pl.when(d <= reach)
            def _():
                rcopy(buf.at[j], buf.at[j], zsend.at[u, side, 0], zrecv.at[u, side, d], dev).wait_recv()

            @pl.when(d < reach)
            def _():
                rcopy(buf.at[j], buf.at[j], zsend.at[u, side, d], zrecv.at[u, side, d + 1], dev).start()

    def ring_end(u):
        buf, reach_r, reach_l = rings[u]

        @pl.loop(0, NZ // 2)
        def _(d):
            for side, reach, dev in ((0, reach_r, dev_zr), (1, reach_l, dev_zl)):
                @pl.when(d < reach)
                def _():
                    rcopy(buf.at[z], buf.at[z], zsend.at[u, side, d], zrecv.at[u, side, 1], dev).wait_send()

    lo, hi = pl.ds(0, HALF), pl.ds(HALF, HALF)
    for slot, dev in ((1, dev_r), (2, dev_l), (0, dev_y), (9, dev_s)):
        send(w_hbm, wall.at[f], slot, dev)
    ring_start(3, do_hbm)
    do_pair = rcopy(do_hbm, pdo, psend.at[4], precv.at[4], dev_p)
    do_pair.start()
    hid_copy = pltpu.make_async_copy(hid_hbm, hid, loc.at[0])
    own_copy = pltpu.make_async_copy(w_hbm, wall.at[f], loc.at[1])
    do_copy = pltpu.make_async_copy(do_hbm, doall.at[z], loc.at[2])
    own_copy.start()
    do_copy.start()
    hid_copy.start()

    ends = []
    total = 0
    for page in range(PAGES):
        total = total + pages[0, page]
        ends.append(total)

    def limits(pos):
        out = jnp.full(pos.shape, NYL * NZ * TOK, jnp.int32)
        for end in ends:
            out = jnp.minimum(out, jnp.where(pos < end, end, NYL * NZ * TOK))
        return out

    lane = lax.broadcasted_iota(jnp.int32, (1, TOK), 1)
    lim_q[:, :TOK] = limits(ctx * TOK + lane)
    lim_q[:, TOK:] = limits(ctx_id(1 - yl, z) * TOK + lane)

    @pl.loop(0, NZ)
    def _(j):
        lim_col[j] = limits(ctx_id(yl, j) * TOK + lane)

    mlu[0:1] = jnp.full((1, 2 * TOK), NEG, F32)
    mlu[1:8] = jnp.zeros((7, 2 * TOK), F32)

    def own(xx, yy):
        return fsdp_id(xx, yy, core)

    def sib(xx, yy):
        return fsdp_id(xx, yy, 1 - core)

    def part(shards):
        out = None
        for s in shards:
            term = nn(hid[:, pl.ds(pl.multiple_of(s * ROWS, ROWS), ROWS)], wall[s])
            out = term if out is None else out + term
        return out

    yc = 1 - yh
    serve(3, 1)
    ol, orr = wall.at[own(left, yh)], wall.at[own(right, yh)]
    arrived(ol, 1)
    on = wall.at[own(left, yh), lo]
    send(on, on, 5, dev_r)
    arrived(orr, 2)
    on = wall.at[own(right, yh), hi]
    send(on, on, 6, dev_l)
    c = wall.at[own(x, yc)]
    arrived(c, 0)
    send(c, c, 3, dev_r)
    send(c, c, 4, dev_l)
    send(ol, ol, 11, dev_s)
    send(orr, orr, 12, dev_s)
    send(c, c, 10, dev_s)
    serve(3, 2)
    hid_copy.wait()
    own_copy.wait()
    do_copy.wait()
    acc[...] = part([f, own(x, yc), own(left, yh), own(right, yh)])
    serve(3, 3)
    fa, fb = wall.at[own(far, yh), lo], wall.at[own(far, yh), hi]
    arrived(fa, 5)
    send(fa, fa, 7, dev_y)
    send(fa, fa, 15, dev_s)
    arrived(fb, 6)
    send(fb, fb, 8, dev_y)
    send(fb, fb, 16, dev_s)
    for slot, ref in (
        (9, wall.at[sib(x, yh)]), (10, wall.at[sib(x, yc)]), (11, wall.at[sib(left, yh)]),
        (12, wall.at[sib(right, yh)]),
    ):
        arrived(ref, slot)
    acc[...] += part([sib(x, yh), sib(x, yc), sib(left, yh), sib(right, yh)])
    serve(3, 4)
    cl, cr = wall.at[own(left, yc)], wall.at[own(right, yc)]
    arrived(cl, 3)
    send(cl, cl, 13, dev_s)
    arrived(cr, 4)
    send(cr, cr, 14, dev_s)
    acc[...] += part([own(left, yc), own(right, yc), own(far, yh)])
    serve(3, 5)
    ca, cb = wall.at[own(far, yc), lo], wall.at[own(far, yc), hi]
    arrived(ca, 7)
    send(ca, ca, 17, dev_s)
    arrived(cb, 8)
    send(cb, cb, 18, dev_s)
    for slot, ref in (
        (13, wall.at[sib(left, yc)]), (14, wall.at[sib(right, yc)]), (15, wall.at[sib(far, yh), lo]),
        (16, wall.at[sib(far, yh), hi]), (17, wall.at[sib(far, yc), lo]), (18, wall.at[sib(far, yc), hi]),
    ):
        arrived(ref, slot)
    acc[...] += part([own(far, yc), sib(left, yc), sib(right, yc), sib(far, yh), sib(far, yc)])
    proj[...] = acc[...].astype(BF16)
    kall[z] = proj[:, HD : 2 * HD]
    vall[z] = proj[:, 2 * HD :]
    ring_start(0, kall.at[z])
    ring_start(1, vall.at[z])
    pair = rcopy(proj, pqkv, psend.at[0], precv.at[0], dev_p)
    pair.start()
    qall[z] = proj[:, :HD]
    wall_copy = pltpu.make_async_copy(wall, wall_out, loc.at[3])
    wall_copy.start()

    q2[:TOK] = proj[:, :HD]
    do2[:TOK] = doall[z]
    do_pair.wait_recv()
    do2[TOK:] = pdo[...]
    serve(3, 6)
    pair.wait_recv()
    q2[TOK:] = pqkv[:, :HD]

    key_row = lax.broadcasted_iota(jnp.int32, (TOK, 1), 0)
    last_q = ctx_id(1, z)

    def score(j, also):
        @pl.when(also & (ctx_id(yl, j) <= last_q + REACH))
        def _():
            s = nt(kall[j], q2[...]) * SCALE
            dp = nt(vall[j], do2[...])
            s = jnp.where(ctx_id(yl, j) * TOK + key_row < lim_q[...], s, NEG)
            s_keep[j] = s
            dp_keep[j] = dp
            m = mlu[0:1]
            m_new = jnp.maximum(m, jnp.max(s, axis=0, keepdims=True))
            p = jnp.exp(s - m_new)
            a = jnp.exp(m - m_new)
            mlu[0:1] = m_new
            mlu[1:2] = mlu[1:2] * a + jnp.sum(p, axis=0, keepdims=True)
            mlu[2:3] = mlu[2:3] * a + jnp.sum(p * dp, axis=0, keepdims=True)

    @pl.loop(1, NZ // 2 + 1)
    def _(k):
        serve(0, k)
        serve(1, k)

        @pl.when(k < 3)
        def _():
            serve(3, k + 6)

        @pl.when(k == LAG)
        def _():
            ring_start(2, qall.at[z])

        @pl.when(k > LAG)
        def _():
            serve(2, k - LAG)

        @pl.loop(0, 2)
        def _(side):
            score((z + NZ - (k - 1) + 2 * (k - 1) * side) % NZ, (side == 0) | (k > 1))

    score((z + NZ // 2) % NZ, True)

    trade = rcopy(mlu, mlu_in, psend.at[1], precv.at[1], dev_p)
    trade.start()
    serve(2, NZ // 2 - LAG + 1)
    trade.wait_recv()

    def merge(mine, theirs):
        m1, m2 = mlu[0:1, mine], mlu_in[0:1, theirs]
        m = jnp.maximum(m1, m2)
        a1, a2 = jnp.exp(m1 - m), jnp.exp(m2 - m)
        l = mlu[1:2, mine] * a1 + mlu_in[1:2, theirs] * a2
        u = mlu[2:3, mine] * a1 + mlu_in[2:3, theirs] * a2
        return m + jnp.log(l), u / l

    own_q, par_q = slice(0, TOK), slice(TOK, 2 * TOK)
    lse_own, dot_own = merge(own_q, par_q)
    lse_par, dot_par = merge(par_q, own_q)
    stats[z, 0:1] = lse_own
    stats[z, 1:2] = dot_own
    stats[z, 2:8] = jnp.zeros((6, TOK), F32)

    @pl.loop(1, NZ)
    def _(i):
        rcopy(stats.at[z], stats.at[z], ssend.at[i], srecv.at[i], at_z(i)).start()

    trade.wait_send()
    mlu[0:1] = jnp.concatenate([lse_own, lse_par], axis=1)
    mlu[1:2] = jnp.concatenate([dot_own, dot_par], axis=1)
    dqt[...] = jnp.zeros((HD, 2 * TOK), F32)

    @pl.loop(0, 4)
    def _(i):
        @pl.loop(0, 4)
        def _(j4):
            j = i * 4 + j4

            @pl.when(ctx_id(yl, j) <= last_q + REACH)
            def _():
                p = jnp.exp(s_keep[j] - mlu[0:1])
                ds = (p * (dp_keep[j] - mlu[1:2]) * SCALE).astype(BF16)
                dqt[...] += tn(kall[j], ds)

        @pl.when(i < LAG - 1)
        def _():
            serve(2, NZ // 2 - LAG + 2 + i)

    out_x[...] = dqt[:, TOK:].astype(BF16)
    dq_copy = rcopy(out_x, in_x, psend.at[2], precv.at[2], dev_p)
    dq_copy.start()

    def keys(src, k_block, wait):
        dkv[...] = jnp.zeros((TOK, 2 * HD), F32)

        @pl.loop(0, NZ)
        def _(i):
            step = (i + 1) // 2
            j = (z + NZ + jnp.where(i % 2 == 1, step, -step)) % NZ
            if wait:
                @pl.when(i > 0)
                def _():
                    d = (z + NZ - j) % NZ
                    rcopy(stats.at[j], stats.at[j], ssend.at[d], srecv.at[d], dev_p).wait_recv()

            @pl.when(k_block <= ctx_id(yl, j) + REACH)
            def _():
                s = nt(src[:, HD : 2 * HD], qall[j]) * SCALE
                dp = nt(src[:, 2 * HD :], doall[j])
                s = jnp.where(k_block * TOK + key_row < lim_col[j], s, NEG)
                p = jnp.exp(s - stats[j, 0:1])
                ds = (p * (dp - stats[j, 1:2]) * SCALE).astype(BF16)
                dkv[:, :HD] += nn(ds, qall[j])
                dkv[:, HD:] += nn(p.astype(BF16), doall[j])

    keys(pqkv, ctx_id(1 - yl, z), True)
    out_kv[...] = dkv[...].astype(BF16)
    kv_copy = rcopy(out_kv, in_kv, psend.at[3], precv.at[3], dev_p)
    kv_copy.start()
    keys(proj, ctx, False)
    dq_copy.wait_recv()
    grad_qkv[:, :HD] = (dqt[:, :TOK] + in_x[...].astype(F32)).T.astype(BF16)
    kv_copy.wait_recv()
    grad_qkv[:, HD:] = (dkv[...] + in_kv[...].astype(F32)).astype(BF16)

    for copy in sent + [do_pair, pair, dq_copy, kv_copy]:
        copy.wait_send()
    for u in range(4):
        ring_end(u)

    @pl.loop(1, NZ)
    def _(d):
        rcopy(stats.at[z], stats.at[z], ssend.at[d], srecv.at[d], dev_p).wait_send()

    wall_copy.wait()


def front(pages, hidden, w, grad_out):
    n = NX * NYH * NC
    any_spec = pl.BlockSpec(memory_space=pl.ANY)
    vmem = pl.BlockSpec(memory_space=pltpu.VMEM)
    dma = pltpu.SemaphoreType.DMA
    return pl.pallas_call(
        front_kernel,
        out_shape=(
            jax.ShapeDtypeStruct((n, ROWS, QKV), BF16),
            jax.ShapeDtypeStruct((TOK, QKV), BF16),
        ),
        in_specs=[pl.BlockSpec(memory_space=pltpu.SMEM)] + [any_spec] * 3,
        out_specs=(any_spec, vmem),
        scratch_shapes=[
            pltpu.VMEM((TOK, D), BF16),
            pltpu.VMEM((n, ROWS, QKV), BF16),
            pltpu.VMEM((TOK, QKV), F32),
            pltpu.VMEM((TOK, QKV), BF16),
            pltpu.VMEM((TOK, QKV), BF16),
            pltpu.VMEM((NZ, TOK, HD), BF16),
            pltpu.VMEM((NZ, TOK, HD), BF16),
            pltpu.VMEM((NZ, TOK, HD), BF16),
            pltpu.VMEM((NZ, TOK, HD), BF16),
            pltpu.VMEM((TOK, HD), BF16),
            pltpu.VMEM((2 * TOK, HD), BF16),
            pltpu.VMEM((2 * TOK, HD), BF16),
            pltpu.VMEM((1, 2 * TOK), jnp.int32),
            pltpu.VMEM((NZ, 1, TOK), jnp.int32),
            pltpu.VMEM((NZ, TOK, 2 * TOK), F32),
            pltpu.VMEM((NZ, TOK, 2 * TOK), F32),
            pltpu.VMEM((8, 2 * TOK), F32),
            pltpu.VMEM((8, 2 * TOK), F32),
            pltpu.VMEM((NZ, 8, TOK), F32),
            pltpu.VMEM((HD, 2 * TOK), F32),
            pltpu.VMEM((TOK, 2 * HD), F32),
            pltpu.VMEM((HD, TOK), BF16),
            pltpu.VMEM((HD, TOK), BF16),
            pltpu.VMEM((TOK, 2 * HD), BF16),
            pltpu.VMEM((TOK, 2 * HD), BF16),
            dma((19,)),
            dma((19,)),
            dma((4, 2, NZ // 2)),
            dma((4, 2, NZ // 2 + 1)),
            dma((5,)),
            dma((5,)),
            dma((NZ,)),
            dma((NZ,)),
            dma((4,)),
        ],
        compiler_params=pltpu.CompilerParams(
            collective_id=0, has_side_effects=True, vmem_limit_bytes=58 << 20
        ),
        name="front",
    )(pages, hidden, w, grad_out)


PATCH = 8
SLICE = ROWS // PATCH


def reduce_kernel(
    hid_hbm, gq, gw_out,
    hid, term, sib, sib_in, got, gotb, relay, total, part, part_in, mid, mid_in, fin, loc, csend, crecv, nsend, nrecv, asend, arecv,
):
    yl, z, x, yh, core = place()
    ctx, f = ctx_id(yl, z), fsdp_id(x, yh, core)
    dev_l, dev_r, dev_y, dev_s = neighbours()
    zl, zh = z % 4, z // 4

    def patch_dev(i):
        return (ctx_id(i // 4, zh * 4 + i % 4), f)

    me = yl * 4 + zl
    peers = [(me + i) % PATCH for i in range(1, PATCH)]
    far_z = [(ctx_id(yl, (z + 4 * i) % NZ), f) for i in range(1, 4)]
    hid_copy = pltpu.make_async_copy(hid_hbm, hid, loc.at[0])
    hid_copy.start()
    greet([dev_l, dev_r, dev_y, dev_s] + [patch_dev(i) for i in peers] + far_z)
    hid_copy.wait()

    n8 = NX * NYH
    lo, hi = pl.ds(0, HALF), pl.ds(HALF, HALF)

    def block(s):
        return tn(hid[:, pl.ds(pl.multiple_of(s * ROWS, ROWS), ROWS)], gq[...])

    left, right, far = (x + NX - 1) % NX, (x + 1) % NX, (x + 2) % NX
    yc = 1 - yh

    def at(xx, yy):
        return xx * NYH + yy

    sent = []

    def send(src, dst, slot, dev):
        copy = rcopy(src, dst, nsend.at[len(sent)], nrecv.at[slot], dev)
        copy.start()
        sent.append(copy)

    def arrived(ref, slot):
        rcopy(ref, ref, nsend.at[0], nrecv.at[slot], dev_s).wait_recv()

    def up(ref):
        return ref[...].astype(F32)

    order = [
        at(far, yc), at(left, yc), at(right, yc), at(far, yh), at(x, yc), at(right, yh), at(left, yh), at(x, yh)
    ]
    for n, i in enumerate(order):
        sib[i] = block(2 * i + 1 - core).astype(BF16)
        rcopy(sib.at[i], sib_in.at[i], csend.at[n], crecv.at[n], dev_s).start()
    for n, i in enumerate(order):
        mine = block(2 * i + core)
        rcopy(sib_in.at[i], sib_in.at[i], csend.at[n], crecv.at[n], dev_s).wait_recv()
        term[i] = (mine + up(sib_in.at[i])).astype(BF16)
        if n < 3:
            to, dev = ((0, dev_y), (2, dev_l), (1, dev_r))[n]
            for h, rows in enumerate((lo, hi)):
                send(term.at[i, rows], got.at[to, rows], 2 * to + h, dev)
    t_far, t_c, t_r, t_l = at(far, yh), at(x, yc), at(right, yh), at(left, yh)
    arrived(got.at[0, lo], 0)
    relay[0, lo] = (up(term.at[t_far, lo]) + up(got.at[0, lo])).astype(BF16)
    send(relay.at[0, lo], gotb.at[0], 12, dev_r)
    arrived(got.at[0, hi], 1)
    relay[0, hi] = (up(term.at[t_far, hi]) + up(got.at[0, hi])).astype(BF16)
    send(relay.at[0, hi], gotb.at[1], 13, dev_l)
    for h, rows in enumerate((lo, hi)):
        arrived(got.at[1, rows], 2 + h)
        arrived(got.at[2, rows], 4 + h)
        relay[1, rows] = (up(term.at[t_c, rows]) + up(got.at[1, rows]) + up(got.at[2, rows])).astype(BF16)
        send(relay.at[1, rows], got.at[5, rows], 10 + h, dev_y)
        if h == 0:
            send(term.at[t_r, hi], got.at[3, hi], 7, dev_r)
            send(term.at[t_l, lo], got.at[4, lo], 8, dev_l)
    arrived(gotb.at[0], 12)
    relay[2, lo] = (up(term.at[t_r, lo]) + up(gotb.at[0])).astype(BF16)
    send(relay.at[2, lo], got.at[3, lo], 6, dev_r)
    arrived(gotb.at[1], 13)
    relay[2, hi] = (up(term.at[t_l, hi]) + up(gotb.at[1])).astype(BF16)
    send(relay.at[2, hi], got.at[4, hi], 9, dev_l)
    for h, rows in enumerate((lo, hi)):
        for slot in (3, 4, 5):
            arrived(got.at[slot, rows], 2 * slot + h)
    total[...] = up(term.at[at(x, yh)]) + up(got.at[3]) + up(got.at[4]) + up(got.at[5])
    part[...] = total[...].astype(BF16).reshape(PATCH, SLICE, QKV)

    for i in range(1, PATCH):
        to = (me + i) % PATCH
        copy = rcopy(part.at[to], part_in.at[i], asend.at[i], arecv.at[i], patch_dev(to))
        copy.start()
        sent.append(copy)
    acc = total[pl.ds(pl.multiple_of(me * SLICE, SLICE), SLICE), :]
    for i in range(1, PATCH):
        rcopy(part_in.at[i], part_in.at[i], asend.at[i], arecv.at[i], dev_s).wait_recv()
        acc += part_in[i].astype(F32)
    mid[...] = acc.astype(BF16)
    for i in range(1, 4):
        copy = rcopy(mid, mid_in.at[i], asend.at[7 + i], arecv.at[7 + i], far_z[i - 1])
        copy.start()
        sent.append(copy)
    for i in range(1, 4):
        rcopy(mid_in.at[i], mid_in.at[i], asend.at[7 + i], arecv.at[7 + i], dev_s).wait_recv()
    mid_in[0] = mid[...]
    acc = jnp.zeros((SLICE, QKV), F32)
    for h in range(4):
        acc += mid_in[(zh - h + 4) % 4].astype(F32)
    fin[me] = acc.astype(BF16)
    for i in range(1, PATCH):
        to = (me + i) % PATCH
        copy = rcopy(fin.at[me], fin.at[me], asend.at[10 + i], arecv.at[10 + i], patch_dev(to))
        copy.start()
        sent.append(copy)
    for i in range(1, PATCH):
        src = fin.at[(me + PATCH - i) % PATCH]
        rcopy(src, src, asend.at[10 + i], arecv.at[10 + i], dev_s).wait_recv()
    gw_out[...] = fin[...].reshape(ROWS, QKV).astype(F32)
    for copy in sent:
        copy.wait_send()

    @pl.loop(0, n8)
    def _(i):
        rcopy(sib.at[i], sib_in.at[i], csend.at[i], crecv.at[i], dev_s).wait_send()


def reduce_weights(hidden, gq):
    n8 = NX * NYH
    vmem = pl.BlockSpec(memory_space=pltpu.VMEM)
    dma = pltpu.SemaphoreType.DMA
    return pl.pallas_call(
        reduce_kernel,
        out_shape=jax.ShapeDtypeStruct((ROWS, QKV), F32),
        in_specs=[pl.BlockSpec(memory_space=pl.ANY), vmem],
        out_specs=vmem,
        scratch_shapes=[
            pltpu.VMEM((TOK, D), BF16),
            pltpu.VMEM((n8, ROWS, QKV), BF16),
            pltpu.VMEM((n8, ROWS, QKV), BF16),
            pltpu.VMEM((n8, ROWS, QKV), BF16),
            pltpu.VMEM((6, ROWS, QKV), BF16),
            pltpu.VMEM((2, HALF, QKV), BF16),
            pltpu.VMEM((3, ROWS, QKV), BF16),
            pltpu.VMEM((ROWS, QKV), F32),
            pltpu.VMEM((PATCH, SLICE, QKV), BF16),
            pltpu.VMEM((PATCH, SLICE, QKV), BF16),
            pltpu.VMEM((SLICE, QKV), BF16),
            pltpu.VMEM((4, SLICE, QKV), BF16),
            pltpu.VMEM((PATCH, SLICE, QKV), BF16),
            dma((1,)),
            dma((n8,)),
            dma((n8,)),
            dma((14,)),
            dma((14,)),
            dma((18,)),
            dma((18,)),
        ],
        compiler_params=pltpu.CompilerParams(
            collective_id=1, has_side_effects=True, vmem_limit_bytes=58 << 20
        ),
        name="reduce_weights",
    )(hidden, gq)


def local(hidden_in, page_tokens, grad_attn, w_qkv):
    hidden = hidden_in[0]
    wall, gq = front(page_tokens, hidden, w_qkv, grad_attn[0])
    grad_w = reduce_weights(hidden, gq)
    grad_hidden = nt(gq, wall.reshape(D, QKV)).astype(BF16)[None]
    return grad_hidden, grad_w


def solution(mesh):
    in_specs = (P("fsdp", "ctx", None), P("fsdp", None), P("fsdp", "ctx", None), P("fsdp", None))
    out_specs = (P("fsdp", "ctx", None), P("fsdp", None))
    return jax.shard_map(local, mesh=mesh, in_specs=in_specs, out_specs=out_specs, check_vma=False)
```

```python
import functools

import jax
import jax.numpy as jnp
from jax import lax
from jax.experimental import pallas as pl
from jax.experimental.pallas import tpu as pltpu
from jax.sharding import PartitionSpec as P

MESH = pl.DeviceIdType.MESH
F32, BF16 = jnp.float32, jnp.bfloat16
NX, NYH, NC, NYL, NZ = 4, 2, 2, 2, 16
TOK, HD, D = 256, 128, 4096
QKV = 3 * HD
ROWS = D // (NX * NYH * NC)
NEG = -1e30
SCALE = HD ** -0.5
LOG2E = 1.4426950408889634
SCALE2 = SCALE * LOG2E
REACH = 5
HALF = TOK // 2
PAGES = 16
LAG = 2
PATCH = 8
SLICE = ROWS // PATCH


def fsdp_id(x, yh, core):
    return (x * NYH + yh) * NC + core


def ctx_id(yl, z):
    return yl * NZ + z


def place():
    ctx, f = lax.axis_index("ctx"), lax.axis_index("fsdp")
    return ctx // NZ, ctx % NZ, f // (NYH * NC), (f // NC) % NYH, f % NC


def rcopy(src, dst, send, recv, dev):
    return pltpu.make_async_remote_copy(
        src_ref=src, dst_ref=dst, send_sem=send, recv_sem=recv, device_id=dev, device_id_type=MESH
    )


def greet(peers):
    barrier = pltpu.get_barrier_semaphore()
    for dev in peers:
        pl.semaphore_signal(barrier, inc=1, device_id=dev, device_id_type=MESH)
    pl.semaphore_wait(barrier, len(peers))


def nt(a, b):
    return lax.dot_general(a, b, (((1,), (1,)), ((), ())), preferred_element_type=F32)


def tn(a, b):
    return lax.dot_general(a, b, (((0,), (0,)), ((), ())), preferred_element_type=F32)


def nn(a, b):
    return jnp.dot(a, b, preferred_element_type=F32)


def neighbours():
    yl, z, x, yh, core = place()
    ctx, f = ctx_id(yl, z), fsdp_id(x, yh, core)
    left, right = (x + NX - 1) % NX, (x + 1) % NX
    dev_l, dev_r = (ctx, fsdp_id(left, yh, core)), (ctx, fsdp_id(right, yh, core))
    dev_y = (ctx_id(1 - yl, z), fsdp_id(x, 1 - yh, core))
    dev_s = (ctx, fsdp_id(x, yh, 1 - core))
    return dev_l, dev_r, dev_y, dev_s


def step_kernel(
    pages, hid_hbm, w_hbm, do_hbm, ghid_out, gw_out,
    hid, wall, acc, proj, pk, pv, kall, vall, qall, doall, pdo, q2, do2, lim_q, lim_col, s_keep, dp_keep, mlu, mlu_in,
    stats, dqt, dkv, out_x, in_x, out_kv, in_kv, wsend, wrecv, zsend, zrecv, psend, precv, ssend, srecv, loc,
    gq, hid_t, ghid, term, sbuf, sbuf_in, got, gotb, relay, total, prt, prt_in, mid, mid_in, fin, csend, crecv, nsend, nrecv, asend, arecv,
):
    yl, z, x, yh, core = place()
    ctx, f = ctx_id(yl, z), fsdp_id(x, yh, core)
    left, right, far = (x + NX - 1) % NX, (x + 1) % NX, (x + 2) % NX
    dev_l, dev_r, dev_y, dev_s = neighbours()
    dev_p = (ctx_id(1 - yl, z), f)

    def at_z(d):
        return (ctx_id(yl, (z + d) % NZ), f)

    dev_zl, dev_zr = at_z(NZ - 1), at_z(1)
    greet([dev_l, dev_r, dev_y, dev_s, dev_p, dev_zl, dev_zr])

    sent = []

    def send(src, dst, slot, dev):
        copy = rcopy(src, dst, wsend.at[len(sent)], wrecv.at[slot], dev)
        copy.start()
        sent.append(copy)

    def arrived(ref, slot):
        rcopy(ref, ref, wsend.at[0], wrecv.at[slot], dev_s).wait_recv()

    rings = ((kall, 8, 7), (vall, 7, 8), (qall, 8, 7), (doall, 7, 8))

    def ring_start(u, src):
        buf = rings[u][0]
        rcopy(src, buf.at[z], zsend.at[u, 0, 0], zrecv.at[u, 0, 1], dev_zr).start()
        rcopy(src, buf.at[z], zsend.at[u, 1, 0], zrecv.at[u, 1, 1], dev_zl).start()

    def serve(u, d):
        buf, reach_r, reach_l = rings[u]
        for side, reach, dev, j in (
            (0, reach_r, dev_zr, (z + NZ - d) % NZ), (1, reach_l, dev_zl, (z + d) % NZ)
        ):
            @pl.when(d <= reach)
            def _():
                rcopy(buf.at[j], buf.at[j], zsend.at[u, side, 0], zrecv.at[u, side, d], dev).wait_recv()

            @pl.when(d < reach)
            def _():
                rcopy(buf.at[j], buf.at[j], zsend.at[u, side, d], zrecv.at[u, side, d + 1], dev).start()

    def ring_end(u):
        buf, reach_r, reach_l = rings[u]

        @pl.loop(0, NZ // 2)
        def _(d):
            for side, reach, dev in ((0, reach_r, dev_zr), (1, reach_l, dev_zl)):
                @pl.when(d < reach)
                def _():
                    rcopy(buf.at[z], buf.at[z], zsend.at[u, side, d], zrecv.at[u, side, 1], dev).wait_send()

    lo, hi = pl.ds(0, HALF), pl.ds(HALF, HALF)
    for slot, rows, dev in ((1, lo, dev_r), (2, hi, dev_l), (19, hi, dev_r), (20, lo, dev_l)):
        send(w_hbm.at[rows], wall.at[f, rows], slot, dev)
    send(w_hbm, wall.at[f], 0, dev_y)
    send(w_hbm, wall.at[f], 9, dev_s)
    ring_start(3, do_hbm)
    do_pair = rcopy(do_hbm, pdo, psend.at[4], precv.at[4], dev_p)
    do_pair.start()
    hid_copy = pltpu.make_async_copy(hid_hbm, hid, loc.at[0])
    own_copy = pltpu.make_async_copy(w_hbm, wall.at[f], loc.at[1])
    do_copy = pltpu.make_async_copy(do_hbm, doall.at[z], loc.at[2])
    own_copy.start()
    do_copy.start()
    hid_copy.start()

    ends = []
    end = 0
    for page in range(PAGES):
        end = end + pages[0, page]
        ends.append(end)

    def limits(pos):
        out = jnp.full(pos.shape, NYL * NZ * TOK, jnp.int32)
        for stop in ends:
            out = jnp.minimum(out, jnp.where(pos < stop, stop, NYL * NZ * TOK))
        return out

    lane = lax.broadcasted_iota(jnp.int32, (1, TOK), 1)
    lim_q[:, :TOK] = limits(ctx * TOK + lane)
    lim_q[:, TOK:] = limits(ctx_id(1 - yl, z) * TOK + lane)

    @pl.loop(0, NZ)
    def _(j):
        lim_col[j] = limits(ctx_id(yl, j) * TOK + lane)

    mlu[0:1] = jnp.full((1, 2 * TOK), NEG, F32)
    mlu[1:8] = jnp.zeros((7, 2 * TOK), F32)

    def own(xx, yy):
        return fsdp_id(xx, yy, core)

    def sib(xx, yy):
        return fsdp_id(xx, yy, 1 - core)

    def project(shards):
        out = None
        for s in shards:
            term = nn(hid[:, pl.ds(pl.multiple_of(s * ROWS, ROWS), ROWS)], wall[s])
            out = term if out is None else out + term
        return out

    yc = 1 - yh
    serve(3, 1)
    ol, orr = wall.at[own(left, yh)], wall.at[own(right, yh)]
    on = wall.at[own(left, yh), lo]
    arrived(on, 1)
    send(on, on, 5, dev_r)
    on = wall.at[own(right, yh), hi]
    arrived(on, 2)
    send(on, on, 6, dev_l)
    c = wall.at[own(x, yc)]
    arrived(c, 0)
    send(c, c, 3, dev_r)
    send(c, c, 4, dev_l)
    arrived(wall.at[own(left, yh), hi], 19)
    send(ol, ol, 11, dev_s)
    arrived(wall.at[own(right, yh), lo], 20)
    send(orr, orr, 12, dev_s)
    send(c, c, 10, dev_s)
    serve(3, 2)
    hid_copy.wait()
    own_copy.wait()
    do_copy.wait()
    acc[...] = project([f, own(x, yc), own(left, yh), own(right, yh)])
    fa, fb = wall.at[own(far, yh), lo], wall.at[own(far, yh), hi]
    arrived(fa, 5)
    send(fa, fa, 7, dev_y)
    send(fa, fa, 15, dev_s)
    arrived(fb, 6)
    send(fb, fb, 8, dev_y)
    send(fb, fb, 16, dev_s)
    serve(3, 3)
    for slot, ref in (
        (9, wall.at[sib(x, yh)]), (10, wall.at[sib(x, yc)]), (11, wall.at[sib(left, yh)]),
        (12, wall.at[sib(right, yh)]),
    ):
        arrived(ref, slot)
    acc[...] += project([sib(x, yh), sib(x, yc), sib(left, yh), sib(right, yh)])
    serve(3, 4)
    cl, cr = wall.at[own(left, yc)], wall.at[own(right, yc)]
    arrived(cl, 3)
    send(cl, cl, 13, dev_s)
    arrived(cr, 4)
    send(cr, cr, 14, dev_s)
    acc[...] += project([own(left, yc), own(right, yc), own(far, yh)])
    ca, cb = wall.at[own(far, yc), lo], wall.at[own(far, yc), hi]
    arrived(ca, 7)
    send(ca, ca, 17, dev_s)
    arrived(cb, 8)
    send(cb, cb, 18, dev_s)
    for slot, ref in (
        (13, wall.at[sib(left, yc)]), (14, wall.at[sib(right, yc)]), (15, wall.at[sib(far, yh), lo]),
        (16, wall.at[sib(far, yh), hi]), (17, wall.at[sib(far, yc), lo]), (18, wall.at[sib(far, yc), hi]),
    ):
        arrived(ref, slot)
    acc[...] += project([own(far, yc), sib(left, yc), sib(right, yc), sib(far, yh), sib(far, yc)])
    proj[...] = acc[...].astype(BF16)
    kall[z] = proj[:, HD : 2 * HD]
    vall[z] = proj[:, 2 * HD :]
    ring_start(0, kall.at[z])
    ring_start(1, vall.at[z])
    qall[z] = proj[:, :HD]
    pair_q = rcopy(qall.at[z], q2.at[pl.ds(TOK, TOK)], psend.at[0], precv.at[0], dev_p)
    pair_q.start()
    pair_k = rcopy(kall.at[z], pk, psend.at[5], precv.at[5], dev_p)
    pair_k.start()
    pair_v = rcopy(vall.at[z], pv, psend.at[6], precv.at[6], dev_p)
    pair_v.start()
    q2[:TOK] = proj[:, :HD]
    do2[:TOK] = doall[z]
    serve(3, 5)

    key_row = lax.broadcasted_iota(jnp.int32, (TOK, 1), 0)
    last_q = ctx_id(1, z)

    def score(j, also):
        @pl.when(also & (ctx_id(yl, j) <= last_q + REACH))
        def _():
            s = nt(kall[j], q2[...]) * SCALE2
            dp = nt(vall[j], do2[...])
            s = jnp.where(ctx_id(yl, j) * TOK + key_row < lim_q[...], s, NEG)
            s_keep[j] = s
            dp_keep[j] = dp
            m = mlu[0:1]
            m_new = jnp.maximum(m, jnp.max(s, axis=0, keepdims=True))
            p = jnp.exp2(s - m_new)
            a = jnp.exp2(m - m_new)
            mlu[0:1] = m_new
            mlu[1:2] = mlu[1:2] * a + jnp.sum(p, axis=0, keepdims=True)
            mlu[2:3] = mlu[2:3] * a + jnp.sum(p * dp, axis=0, keepdims=True)

    @pl.loop(1, NZ // 2 + 1)
    def _(k):
        serve(0, k)
        serve(1, k)

        @pl.when(k < 4)
        def _():
            serve(3, k + 5)

        @pl.when(k == 1)
        def _():
            do_pair.wait_recv()
            do2[TOK:] = pdo[...]
            pair_q.wait_recv()

        @pl.when(k == LAG)
        def _():
            ring_start(2, qall.at[z])

        @pl.when(k > LAG)
        def _():
            serve(2, k - LAG)

        @pl.loop(0, 2)
        def _(side):
            score((z + NZ - (k - 1) + 2 * (k - 1) * side) % NZ, (side == 0) | (k > 1))
            n = 2 * (k - 1) + side
            hid_t[n] = hid[:, pl.ds(pl.multiple_of(n * ROWS, ROWS), ROWS)].T

    score((z + NZ // 2) % NZ, True)

    trade = rcopy(mlu, mlu_in, psend.at[1], precv.at[1], dev_p)
    trade.start()
    serve(2, NZ // 2 - LAG + 1)
    trade.wait_recv()

    def merge(mine, theirs):
        m1, m2 = mlu[0:1, mine], mlu_in[0:1, theirs]
        m = jnp.maximum(m1, m2)
        a1, a2 = jnp.exp2(m1 - m), jnp.exp2(m2 - m)
        l = mlu[1:2, mine] * a1 + mlu_in[1:2, theirs] * a2
        u = mlu[2:3, mine] * a1 + mlu_in[2:3, theirs] * a2
        return m + jnp.log(l) * LOG2E, u / l

    own_q, par_q = slice(0, TOK), slice(TOK, 2 * TOK)
    lse_own, dot_own = merge(own_q, par_q)
    lse_par, dot_par = merge(par_q, own_q)
    stats[z, :, :TOK] = lse_own
    stats[z, :, TOK:] = dot_own

    @pl.loop(1, NZ)
    def _(i):
        rcopy(stats.at[z], stats.at[z], ssend.at[i], srecv.at[i], at_z(i)).start()

    trade.wait_send()
    mlu[0:1] = jnp.concatenate([lse_own, lse_par], axis=1)
    mlu[1:2] = jnp.concatenate([dot_own, dot_par], axis=1)
    dqt[...] = jnp.zeros((HD, 2 * TOK), F32)

    @pl.loop(0, NZ // 4)
    def _(i):
        @pl.when(ctx_id(yl, 4 * i) <= last_q + REACH)
        def _():
            for n in range(1, 4):
                @pl.when(ctx_id(yl, 4 * i + n) > last_q + REACH)
                def _():
                    s_keep[4 * i + n] = jnp.full((TOK, 2 * TOK), NEG, F32)
                    dp_keep[4 * i + n] = jnp.zeros((TOK, 2 * TOK), F32)

            out = []
            for n in range(4):
                j = 4 * i + n
                p = jnp.exp2(s_keep[j] - mlu[0:1])
                ds = (p * (dp_keep[j] - mlu[1:2])).astype(BF16)
                out.append(tn(kall[j], ds))
            dqt[...] += (out[0] + out[1]) + (out[2] + out[3])

        @pl.when((i == 1) & (LAG > 1))
        def _():
            serve(2, NZ // 2)

    dqt[...] = dqt[...] * SCALE
    out_x[...] = dqt[:, TOK:].astype(BF16)
    dq_copy = rcopy(out_x, in_x, psend.at[2], precv.at[2], dev_p)
    dq_copy.start()

    def keys(k_src, v_src, k_block, wait):
        dkv[...] = jnp.zeros((TOK, 2 * HD), F32)

        def arrive(j):
            n = (z + NZ - j) % NZ
            rcopy(stats.at[j], stats.at[j], ssend.at[n], srecv.at[n], dev_p).wait_recv()

        def work(blocks):
            seen = k_block <= ctx_id(yl, blocks[0]) + REACH
            for j in blocks[1:]:
                seen = seen | (k_block <= ctx_id(yl, j) + REACH)

            @pl.when(seen)
            def _():
                dk, dv = [], []
                for j in blocks:
                    s = nt(k_src[...], qall[j]) * SCALE2
                    dp = nt(v_src[...], doall[j])
                    s = jnp.where(k_block * TOK + key_row < lim_col[j], s, NEG)
                    p = jnp.exp2(s - stats[j, :, :TOK])
                    ds = (p * (dp - stats[j, :, TOK:])).astype(BF16)
                    dk.append(nn(ds, qall[j]))
                    dv.append(nn(p.astype(BF16), doall[j]))
                dkv[:, :HD] += sum(dk[1:], dk[0])
                dkv[:, HD:] += sum(dv[1:], dv[0])

        work([z])

        @pl.loop(0, NZ // 4 - 1)
        def _(i):
            near = [(z + NZ - 2 * i - 1) % NZ, (z + 2 * i + 1) % NZ, (z + NZ - 2 * i - 2) % NZ, (z + 2 * i + 2) % NZ]
            if wait:
                for j in near:
                    arrive(j)
            work(near)

        last = [(z + NZ // 2 + 1) % NZ, (z + NZ // 2 - 1) % NZ, (z + NZ // 2) % NZ]
        if wait:
            for j in last:
                arrive(j)
        work(last)
        dkv[:, :HD] = dkv[:, :HD] * SCALE

    pair_k.wait_recv()
    pair_v.wait_recv()
    keys(pk, pv, ctx_id(1 - yl, z), True)
    out_kv[...] = dkv[...].astype(BF16)
    kv_copy = rcopy(out_kv, in_kv, psend.at[3], precv.at[3], dev_p)
    kv_copy.start()
    dq_copy.wait_recv()
    gq[:, :HD] = (dqt[:, :TOK] + in_x[...].astype(F32)).T.astype(BF16)
    keys(kall.at[z], vall.at[z], ctx, False)
    kv_copy.wait_recv()
    gq[:, HD:] = (dkv[...] + in_kv[...].astype(F32)).astype(BF16)

    zl, zh = z % 4, z // 4

    def patch_dev(i):
        return (ctx_id(i // 4, zh * 4 + i % 4), f)

    me = yl * 4 + zl
    far_z = [(ctx_id(yl, (z + 4 * i) % NZ), f) for i in range(1, 4)]

    n8 = NX * NYH

    def grad_in(first):
        for s in range(first, first + 4):
            ghid[:, s * ROWS : (s + 1) * ROWS] = nt(gq[...], wall[s]).astype(BF16)
        cols = pl.ds(first * ROWS, 4 * ROWS)
        pltpu.make_async_copy(ghid.at[:, cols], ghid_out.at[:, cols], loc.at[3 + first // 4]).start()

    def block(s):
        return nn(hid_t[s], gq[...])

    def at(xx, yy):
        return xx * NYH + yy

    rsent = []

    def rsend(src, dst, slot, dev):
        copy = rcopy(src, dst, nsend.at[len(rsent)], nrecv.at[slot], dev)
        copy.start()
        rsent.append(copy)

    def rarrived(ref, slot):
        rcopy(ref, ref, nsend.at[0], nrecv.at[slot], dev_s).wait_recv()

    def up(ref):
        return ref[...].astype(F32)

    order = [
        at(far, yc), at(left, yc), at(right, yc), at(far, yh), at(x, yc), at(right, yh), at(left, yh), at(x, yh)
    ]
    for n, i in enumerate(order):
        sbuf[i] = block(2 * i + 1 - core).astype(BF16)
        rcopy(sbuf.at[i], sbuf_in.at[i], csend.at[n], crecv.at[n], dev_s).start()
    for n, i in enumerate(order):
        mine = block(2 * i + core)
        rcopy(sbuf_in.at[i], sbuf_in.at[i], csend.at[n], crecv.at[n], dev_s).wait_recv()
        term[i] = (mine + up(sbuf_in.at[i])).astype(BF16)
        if n < 3:
            to, dev = ((0, dev_y), (2, dev_l), (1, dev_r))[n]
            for h, rows in enumerate((lo, hi)):
                rsend(term.at[i, rows], got.at[to, rows], 2 * to + h, dev)
    grad_in(0)
    t_far, t_c, t_r, t_l = at(far, yh), at(x, yc), at(right, yh), at(left, yh)
    rarrived(got.at[0, lo], 0)
    relay[0, lo] = (up(term.at[t_far, lo]) + up(got.at[0, lo])).astype(BF16)
    rsend(relay.at[0, lo], gotb.at[0], 12, dev_r)
    rarrived(got.at[0, hi], 1)
    relay[0, hi] = (up(term.at[t_far, hi]) + up(got.at[0, hi])).astype(BF16)
    rsend(relay.at[0, hi], gotb.at[1], 13, dev_l)
    for h, rows in enumerate((lo, hi)):
        rarrived(got.at[1, rows], 2 + h)
        rarrived(got.at[2, rows], 4 + h)
        relay[1, rows] = (up(term.at[t_c, rows]) + up(got.at[1, rows]) + up(got.at[2, rows])).astype(BF16)
        rsend(relay.at[1, rows], got.at[5, rows], 10 + h, dev_y)
        if h == 0:
            rsend(term.at[t_r, hi], got.at[3, hi], 7, dev_r)
            rsend(term.at[t_l, lo], got.at[4, lo], 8, dev_l)
    rarrived(gotb.at[0], 12)
    relay[2, lo] = (up(term.at[t_r, lo]) + up(gotb.at[0])).astype(BF16)
    rsend(relay.at[2, lo], got.at[3, lo], 6, dev_r)
    rarrived(gotb.at[1], 13)
    relay[2, hi] = (up(term.at[t_l, hi]) + up(gotb.at[1])).astype(BF16)
    rsend(relay.at[2, hi], got.at[4, hi], 9, dev_l)
    for h, rows in enumerate((lo, hi)):
        for slot in (3, 4, 5):
            rarrived(got.at[slot, rows], 2 * slot + h)
    total[...] = up(term.at[at(x, yh)]) + up(got.at[3]) + up(got.at[4]) + up(got.at[5])
    prt[...] = total[...].astype(BF16).reshape(PATCH, SLICE, QKV)

    for i in range(1, PATCH):
        to = (me + i) % PATCH
        copy = rcopy(prt.at[to], prt_in.at[i], asend.at[i], arecv.at[i], patch_dev(to))
        copy.start()
        rsent.append(copy)
    grad_in(4)
    run = total[pl.ds(pl.multiple_of(me * SLICE, SLICE), SLICE), :]
    for i in range(1, PATCH):
        rcopy(prt_in.at[i], prt_in.at[i], asend.at[i], arecv.at[i], dev_s).wait_recv()
        run += prt_in[i].astype(F32)
    mid[...] = run.astype(BF16)
    for i in range(1, 4):
        copy = rcopy(mid, mid_in.at[i], asend.at[7 + i], arecv.at[7 + i], far_z[i - 1])
        copy.start()
        rsent.append(copy)
    grad_in(8)
    for i in range(1, 4):
        rcopy(mid_in.at[i], mid_in.at[i], asend.at[7 + i], arecv.at[7 + i], dev_s).wait_recv()
    mid_in[0] = mid[...]
    run = jnp.zeros((SLICE, QKV), F32)
    for h in range(4):
        run += mid_in[(zh - h + 4) % 4].astype(F32)
    fin[me] = run.astype(BF16)
    for i in range(1, PATCH):
        to = (me + i) % PATCH
        copy = rcopy(fin.at[me], fin.at[me], asend.at[10 + i], arecv.at[10 + i], patch_dev(to))
        copy.start()
        rsent.append(copy)
    grad_in(12)
    for i in range(1, PATCH):
        src = fin.at[(me + PATCH - i) % PATCH]
        rcopy(src, src, asend.at[10 + i], arecv.at[10 + i], dev_s).wait_recv()
    gw_out[...] = fin[...].reshape(ROWS, QKV).astype(F32)
    for copy in sent + rsent + [do_pair, pair_q, pair_k, pair_v, dq_copy, kv_copy]:
        copy.wait_send()
    for u in range(4):
        ring_end(u)

    @pl.loop(1, NZ)
    def _(d):
        rcopy(stats.at[z], stats.at[z], ssend.at[d], srecv.at[d], dev_p).wait_send()

    @pl.loop(0, n8)
    def _(i):
        rcopy(sbuf.at[i], sbuf_in.at[i], csend.at[i], crecv.at[i], dev_s).wait_send()

    for first in range(0, NX * NYH * NC, 4):
        cols = pl.ds(first * ROWS, 4 * ROWS)
        pltpu.make_async_copy(ghid.at[:, cols], ghid_out.at[:, cols], loc.at[3 + first // 4]).wait()


def step(pages, hidden, w, grad_out):
    n, n8 = NX * NYH * NC, NX * NYH
    hbm = pl.BlockSpec(memory_space=pltpu.HBM)
    vmem = pl.BlockSpec(memory_space=pltpu.VMEM)
    dma = pltpu.SemaphoreType.DMA
    return pl.pallas_call(
        step_kernel,
        out_shape=(
            jax.ShapeDtypeStruct((TOK, D), BF16),
            jax.ShapeDtypeStruct((ROWS, QKV), F32),
        ),
        in_specs=[pl.BlockSpec(memory_space=pltpu.SMEM)] + [hbm] * 3,
        out_specs=(hbm, vmem),
        scratch_shapes=[
            pltpu.VMEM((TOK, D), BF16),
            pltpu.VMEM((n, ROWS, QKV), BF16),
            pltpu.VMEM((TOK, QKV), F32),
            pltpu.VMEM((TOK, QKV), BF16),
            pltpu.VMEM((TOK, HD), BF16),
            pltpu.VMEM((TOK, HD), BF16),
            pltpu.VMEM((NZ, TOK, HD), BF16),
            pltpu.VMEM((NZ, TOK, HD), BF16),
            pltpu.VMEM((NZ, TOK, HD), BF16),
            pltpu.VMEM((NZ, TOK, HD), BF16),
            pltpu.VMEM((TOK, HD), BF16),
            pltpu.VMEM((2 * TOK, HD), BF16),
            pltpu.VMEM((2 * TOK, HD), BF16),
            pltpu.VMEM((1, 2 * TOK), jnp.int32),
            pltpu.VMEM((NZ, 1, TOK), jnp.int32),
            pltpu.VMEM((NZ, TOK, 2 * TOK), F32),
            pltpu.VMEM((NZ, TOK, 2 * TOK), F32),
            pltpu.VMEM((8, 2 * TOK), F32),
            pltpu.VMEM((8, 2 * TOK), F32),
            pltpu.VMEM((NZ, 1, 2 * TOK), F32),
            pltpu.VMEM((HD, 2 * TOK), F32),
            pltpu.VMEM((TOK, 2 * HD), F32),
            pltpu.VMEM((HD, TOK), BF16),
            pltpu.VMEM((HD, TOK), BF16),
            pltpu.VMEM((TOK, 2 * HD), BF16),
            pltpu.VMEM((TOK, 2 * HD), BF16),
            dma((21,)),
            dma((21,)),
            dma((4, 2, NZ // 2)),
            dma((4, 2, NZ // 2 + 1)),
            dma((7,)),
            dma((7,)),
            dma((NZ,)),
            dma((NZ,)),
            dma((7,)),
            pltpu.VMEM((TOK, QKV), BF16),
            pltpu.VMEM((n, ROWS, TOK), BF16),
            pltpu.VMEM((TOK, D), BF16),
            pltpu.VMEM((n8, ROWS, QKV), BF16),
            pltpu.VMEM((n8, ROWS, QKV), BF16),
            pltpu.VMEM((n8, ROWS, QKV), BF16),
            pltpu.VMEM((6, ROWS, QKV), BF16),
            pltpu.VMEM((2, HALF, QKV), BF16),
            pltpu.VMEM((3, ROWS, QKV), BF16),
            pltpu.VMEM((ROWS, QKV), F32),
            pltpu.VMEM((PATCH, SLICE, QKV), BF16),
            pltpu.VMEM((PATCH, SLICE, QKV), BF16),
            pltpu.VMEM((SLICE, QKV), BF16),
            pltpu.VMEM((4, SLICE, QKV), BF16),
            pltpu.VMEM((PATCH, SLICE, QKV), BF16),
            dma((n8,)),
            dma((n8,)),
            dma((14,)),
            dma((14,)),
            dma((18,)),
            dma((18,)),
        ],
        compiler_params=pltpu.CompilerParams(
            collective_id=0, has_side_effects=True, vmem_limit_bytes=60 << 20
        ),
        name="step",
    )(pages, hidden, w, grad_out)


def local(hidden_in, page_tokens, grad_attn, w_qkv):
    grad_hidden, grad_w = step(page_tokens, hidden_in[0], w_qkv, grad_attn[0])
    return grad_hidden[None], grad_w


def solution(mesh):
    in_specs = (P("fsdp", "ctx", None), P("fsdp", None), P("fsdp", "ctx", None), P("fsdp", None))
    out_specs = (P("fsdp", "ctx", None), P("fsdp", None))
    return jax.shard_map(local, mesh=mesh, in_specs=in_specs, out_specs=out_specs, check_vma=False)
```

```python
import functools

import jax
import jax.numpy as jnp
from jax import lax
from jax.experimental import pallas as pl
from jax.experimental.pallas import tpu as pltpu
from jax.sharding import PartitionSpec as P

MESH = pl.DeviceIdType.MESH
F32, BF16 = jnp.float32, jnp.bfloat16
NX, NYH, NC, NYL, NZ = 4, 2, 2, 2, 16
TOK, HD, D = 256, 128, 4096
QKV = 3 * HD
ROWS = D // (NX * NYH * NC)
NEG = -1e30
SCALE = HD ** -0.5
LOG2E = 1.4426950408889634
SCALE2 = SCALE * LOG2E
REACH = 5
WRITES = 8
HALF = TOK // 2
PAGES = 16
LAG = 2
PATCH = 8
SLICE = ROWS // PATCH


def fsdp_id(x, yh, core):
    return (x * NYH + yh) * NC + core


def ctx_id(yl, z):
    return yl * NZ + z


def place():
    ctx, f = lax.axis_index("ctx"), lax.axis_index("fsdp")
    return ctx // NZ, ctx % NZ, f // (NYH * NC), (f // NC) % NYH, f % NC


def rcopy(src, dst, send, recv, dev):
    return pltpu.make_async_remote_copy(
        src_ref=src, dst_ref=dst, send_sem=send, recv_sem=recv, device_id=dev, device_id_type=MESH
    )


def greet(peers):
    barrier = pltpu.get_barrier_semaphore()
    for dev in peers:
        pl.semaphore_signal(barrier, inc=1, device_id=dev, device_id_type=MESH)
    pl.semaphore_wait(barrier, len(peers))


def nt(a, b):
    return lax.dot_general(a, b, (((1,), (1,)), ((), ())), preferred_element_type=F32)


def tn(a, b):
    return lax.dot_general(a, b, (((0,), (0,)), ((), ())), preferred_element_type=F32)


def nn(a, b):
    return jnp.dot(a, b, preferred_element_type=F32)


def neighbours():
    yl, z, x, yh, core = place()
    ctx, f = ctx_id(yl, z), fsdp_id(x, yh, core)
    left, right = (x + NX - 1) % NX, (x + 1) % NX
    dev_l, dev_r = (ctx, fsdp_id(left, yh, core)), (ctx, fsdp_id(right, yh, core))
    dev_y = (ctx_id(1 - yl, z), fsdp_id(x, 1 - yh, core))
    dev_s = (ctx, fsdp_id(x, yh, 1 - core))
    return dev_l, dev_r, dev_y, dev_s


def step_kernel(
    pages, hid_hbm, w_hbm, do_hbm, ghid_out, gw_out,
    hid, wall, acc, proj, pk, pv, kall, vall, qall, doall, pdo, q2, do2, lim_q, lim_col, s_keep, dp_keep, mlu, mlu_in,
    stats, dqt, dkv, out_x, in_x, out_kv, in_kv, wsend, wrecv, zsend, zrecv, psend, precv, ssend, srecv, loc,
    gq, hid_t, ghid, term, sbuf, sbuf_in, got, gotb, relay, total, prt, prt_in, mid, mid_in, fin, csend, crecv, nsend, nrecv, asend, arecv,
):
    yl, z, x, yh, core = place()
    ctx, f = ctx_id(yl, z), fsdp_id(x, yh, core)
    left, right, far = (x + NX - 1) % NX, (x + 1) % NX, (x + 2) % NX
    dev_l, dev_r, dev_y, dev_s = neighbours()
    dev_p = (ctx_id(1 - yl, z), f)

    def at_z(d):
        return (ctx_id(yl, (z + d) % NZ), f)

    dev_zl, dev_zr = at_z(NZ - 1), at_z(1)
    greet([dev_l, dev_r, dev_y, dev_s, dev_p, dev_zl, dev_zr])

    sent = []

    def send(src, dst, slot, dev):
        copy = rcopy(src, dst, wsend.at[len(sent)], wrecv.at[slot], dev)
        copy.start()
        sent.append(copy)

    def arrived(ref, slot):
        rcopy(ref, ref, wsend.at[0], wrecv.at[slot], dev_s).wait_recv()

    rings = ((kall, 8, 7), (vall, 7, 8), (qall, 8, 7), (doall, 7, 8))

    def ring_start(u, src):
        buf = rings[u][0]
        rcopy(src, buf.at[z], zsend.at[u, 0, 0], zrecv.at[u, 0, 1], dev_zr).start()
        rcopy(src, buf.at[z], zsend.at[u, 1, 0], zrecv.at[u, 1, 1], dev_zl).start()

    def serve(u, d):
        buf, reach_r, reach_l = rings[u]
        for side, reach, dev, j in (
            (0, reach_r, dev_zr, (z + NZ - d) % NZ), (1, reach_l, dev_zl, (z + d) % NZ)
        ):
            @pl.when(d <= reach)
            def _():
                rcopy(buf.at[j], buf.at[j], zsend.at[u, side, 0], zrecv.at[u, side, d], dev).wait_recv()

            @pl.when(d < reach)
            def _():
                rcopy(buf.at[j], buf.at[j], zsend.at[u, side, d], zrecv.at[u, side, d + 1], dev).start()

    def ring_end(u):
        buf, reach_r, reach_l = rings[u]

        @pl.loop(0, NZ // 2)
        def _(d):
            for side, reach, dev in ((0, reach_r, dev_zr), (1, reach_l, dev_zl)):
                @pl.when(d < reach)
                def _():
                    rcopy(buf.at[z], buf.at[z], zsend.at[u, side, d], zrecv.at[u, side, 1], dev).wait_send()

    lo, hi = pl.ds(0, HALF), pl.ds(HALF, HALF)
    for slot, rows, dev in ((1, lo, dev_r), (2, hi, dev_l), (19, hi, dev_r), (20, lo, dev_l)):
        send(w_hbm.at[rows], wall.at[f, rows], slot, dev)
    send(w_hbm, wall.at[f], 0, dev_y)
    send(w_hbm, wall.at[f], 9, dev_s)
    ring_start(3, do_hbm)
    do_pair = rcopy(do_hbm, pdo, psend.at[4], precv.at[4], dev_p)
    do_pair.start()
    hid_copy = pltpu.make_async_copy(hid_hbm, hid, loc.at[0])
    own_copy = pltpu.make_async_copy(w_hbm, wall.at[f], loc.at[1])
    do_copy = pltpu.make_async_copy(do_hbm, doall.at[z], loc.at[2])
    own_copy.start()
    do_copy.start()
    hid_copy.start()

    ends = []
    end = 0
    for page in range(PAGES):
        end = end + pages[0, page]
        ends.append(end)

    def limits(pos):
        out = jnp.full(pos.shape, NYL * NZ * TOK, jnp.int32)
        for stop in ends:
            out = jnp.minimum(out, jnp.where(pos < stop, stop, NYL * NZ * TOK))
        return out

    lane = lax.broadcasted_iota(jnp.int32, (1, TOK), 1)
    lim_q[:, :TOK] = limits(ctx * TOK + lane)
    lim_q[:, TOK:] = limits(ctx_id(1 - yl, z) * TOK + lane)

    @pl.loop(0, NZ)
    def _(j):
        lim_col[j] = limits(ctx_id(yl, j) * TOK + lane)

    mlu[0:1] = jnp.full((1, 2 * TOK), NEG, F32)
    mlu[1:8] = jnp.zeros((7, 2 * TOK), F32)

    def own(xx, yy):
        return fsdp_id(xx, yy, core)

    def sib(xx, yy):
        return fsdp_id(xx, yy, 1 - core)

    def project(shards):
        out = None
        for s in shards:
            term = nn(hid[:, pl.ds(pl.multiple_of(s * ROWS, ROWS), ROWS)], wall[s])
            out = term if out is None else out + term
        return out

    yc = 1 - yh
    serve(3, 1)
    ol, orr = wall.at[own(left, yh)], wall.at[own(right, yh)]
    on = wall.at[own(left, yh), lo]
    arrived(on, 1)
    send(on, on, 5, dev_r)
    on = wall.at[own(right, yh), hi]
    arrived(on, 2)
    send(on, on, 6, dev_l)
    c = wall.at[own(x, yc)]
    arrived(c, 0)
    send(c, c, 3, dev_r)
    send(c, c, 4, dev_l)
    arrived(wall.at[own(left, yh), hi], 19)
    send(ol, ol, 11, dev_s)
    arrived(wall.at[own(right, yh), lo], 20)
    send(orr, orr, 12, dev_s)
    send(c, c, 10, dev_s)
    serve(3, 2)
    hid_copy.wait()
    own_copy.wait()
    do_copy.wait()
    acc[...] = project([f, own(x, yc), own(left, yh), own(right, yh)])
    fa, fb = wall.at[own(far, yh), lo], wall.at[own(far, yh), hi]
    arrived(fa, 5)
    send(fa, fa, 7, dev_y)
    send(fa, fa, 15, dev_s)
    arrived(fb, 6)
    send(fb, fb, 8, dev_y)
    send(fb, fb, 16, dev_s)
    serve(3, 3)
    for slot, ref in (
        (9, wall.at[sib(x, yh)]), (10, wall.at[sib(x, yc)]), (11, wall.at[sib(left, yh)]),
        (12, wall.at[sib(right, yh)]),
    ):
        arrived(ref, slot)
    acc[...] += project([sib(x, yh), sib(x, yc), sib(left, yh), sib(right, yh)])
    serve(3, 4)
    cl, cr = wall.at[own(left, yc)], wall.at[own(right, yc)]
    arrived(cl, 3)
    send(cl, cl, 13, dev_s)
    arrived(cr, 4)
    send(cr, cr, 14, dev_s)
    acc[...] += project([own(left, yc), own(right, yc), own(far, yh)])
    ca, cb = wall.at[own(far, yc), lo], wall.at[own(far, yc), hi]
    arrived(ca, 7)
    send(ca, ca, 17, dev_s)
    arrived(cb, 8)
    send(cb, cb, 18, dev_s)
    for slot, ref in (
        (13, wall.at[sib(left, yc)]), (14, wall.at[sib(right, yc)]), (15, wall.at[sib(far, yh), lo]),
        (16, wall.at[sib(far, yh), hi]), (17, wall.at[sib(far, yc), lo]), (18, wall.at[sib(far, yc), hi]),
    ):
        arrived(ref, slot)
    acc[...] += project([own(far, yc), sib(left, yc), sib(right, yc), sib(far, yh), sib(far, yc)])
    proj[...] = acc[...].astype(BF16)
    kall[z] = proj[:, HD : 2 * HD]
    vall[z] = proj[:, 2 * HD :]
    ring_start(0, kall.at[z])
    ring_start(1, vall.at[z])
    qall[z] = proj[:, :HD]
    pair_q = rcopy(qall.at[z], q2.at[pl.ds(TOK, TOK)], psend.at[0], precv.at[0], dev_p)
    pair_q.start()
    pair_k = rcopy(kall.at[z], pk, psend.at[5], precv.at[5], dev_p)
    pair_k.start()
    pair_v = rcopy(vall.at[z], pv, psend.at[6], precv.at[6], dev_p)
    pair_v.start()
    q2[:TOK] = proj[:, :HD]
    do2[:TOK] = doall[z]
    serve(3, 5)

    key_row = lax.broadcasted_iota(jnp.int32, (TOK, 1), 0)
    last_q = ctx_id(1, z)

    def score(j, also):
        @pl.when(also & (ctx_id(yl, j) <= last_q + REACH))
        def _():
            s = nt(kall[j], q2[...]) * SCALE2
            dp = nt(vall[j], do2[...])
            s = jnp.where(ctx_id(yl, j) * TOK + key_row < lim_q[...], s, NEG)
            s_keep[j] = s
            dp_keep[j] = dp
            m = mlu[0:1]
            m_new = jnp.maximum(m, jnp.max(s, axis=0, keepdims=True))
            p = jnp.exp2(s - m_new)
            a = jnp.exp2(m - m_new)
            mlu[0:1] = m_new
            mlu[1:2] = mlu[1:2] * a + jnp.sum(p, axis=0, keepdims=True)
            mlu[2:3] = mlu[2:3] * a + jnp.sum(p * dp, axis=0, keepdims=True)

    @pl.loop(1, NZ // 2 + 1)
    def _(k):
        serve(0, k)
        serve(1, k)

        @pl.when(k < 4)
        def _():
            serve(3, k + 5)

        @pl.when(k == 1)
        def _():
            do_pair.wait_recv()
            do2[TOK:] = pdo[...]
            pair_q.wait_recv()

        @pl.when(k == LAG)
        def _():
            ring_start(2, qall.at[z])

        @pl.when(k > LAG)
        def _():
            serve(2, k - LAG)

        @pl.loop(0, 2)
        def _(side):
            score((z + NZ - (k - 1) + 2 * (k - 1) * side) % NZ, (side == 0) | (k > 1))
            n = 2 * (k - 1) + side
            hid_t[n] = hid[:, pl.ds(pl.multiple_of(n * ROWS, ROWS), ROWS)].T

    score((z + NZ // 2) % NZ, True)

    trade = rcopy(mlu, mlu_in, psend.at[1], precv.at[1], dev_p)
    trade.start()
    serve(2, NZ // 2 - LAG + 1)
    trade.wait_recv()

    def merge(mine, theirs):
        m1, m2 = mlu[0:1, mine], mlu_in[0:1, theirs]
        m = jnp.maximum(m1, m2)
        a1, a2 = jnp.exp2(m1 - m), jnp.exp2(m2 - m)
        l = mlu[1:2, mine] * a1 + mlu_in[1:2, theirs] * a2
        u = mlu[2:3, mine] * a1 + mlu_in[2:3, theirs] * a2
        return m + jnp.log(l) * LOG2E, u / l

    own_q, par_q = slice(0, TOK), slice(TOK, 2 * TOK)
    lse_own, dot_own = merge(own_q, par_q)
    lse_par, dot_par = merge(par_q, own_q)
    stats[z, :, :TOK] = lse_own
    stats[z, :, TOK:] = dot_own

    @pl.loop(1, NZ)
    def _(i):
        rcopy(stats.at[z], stats.at[z], ssend.at[i], srecv.at[i], at_z(i)).start()

    trade.wait_send()
    mlu[0:1] = jnp.concatenate([lse_own, lse_par], axis=1)
    mlu[1:2] = jnp.concatenate([dot_own, dot_par], axis=1)
    dqt[...] = jnp.zeros((HD, 2 * TOK), F32)

    @pl.loop(0, NZ // 4)
    def _(i):
        @pl.when(ctx_id(yl, 4 * i) <= last_q + REACH)
        def _():
            for n in range(1, 4):
                @pl.when(ctx_id(yl, 4 * i + n) > last_q + REACH)
                def _():
                    s_keep[4 * i + n] = jnp.full((TOK, 2 * TOK), NEG, F32)
                    dp_keep[4 * i + n] = jnp.zeros((TOK, 2 * TOK), F32)

            out = []
            for n in range(4):
                j = 4 * i + n
                p = jnp.exp2(s_keep[j] - mlu[0:1])
                ds = (p * (dp_keep[j] - mlu[1:2])).astype(BF16)
                out.append(tn(kall[j], ds))
            dqt[...] += (out[0] + out[1]) + (out[2] + out[3])

        @pl.when((i == 1) & (LAG > 1))
        def _():
            serve(2, NZ // 2)

    dqt[...] = dqt[...] * SCALE
    out_x[...] = dqt[:, TOK:].astype(BF16)
    dq_copy = rcopy(out_x, in_x, psend.at[2], precv.at[2], dev_p)
    dq_copy.start()

    def keys(k_src, v_src, k_block, wait):
        dkv[...] = jnp.zeros((TOK, 2 * HD), F32)

        def arrive(j):
            n = (z + NZ - j) % NZ
            rcopy(stats.at[j], stats.at[j], ssend.at[n], srecv.at[n], dev_p).wait_recv()

        def work(blocks):
            seen = k_block <= ctx_id(yl, blocks[0]) + REACH
            for j in blocks[1:]:
                seen = seen | (k_block <= ctx_id(yl, j) + REACH)

            @pl.when(seen)
            def _():
                dk, dv = [], []
                for j in blocks:
                    s = nt(k_src[...], qall[j]) * SCALE2
                    dp = nt(v_src[...], doall[j])
                    s = jnp.where(k_block * TOK + key_row < lim_col[j], s, NEG)
                    p = jnp.exp2(s - stats[j, :, :TOK])
                    ds = (p * (dp - stats[j, :, TOK:])).astype(BF16)
                    dk.append(nn(ds, qall[j]))
                    dv.append(nn(p.astype(BF16), doall[j]))
                dkv[:, :HD] += sum(dk[1:], dk[0])
                dkv[:, HD:] += sum(dv[1:], dv[0])

        work([z])

        @pl.loop(0, NZ // 4 - 1)
        def _(i):
            near = [(z + NZ - 2 * i - 1) % NZ, (z + 2 * i + 1) % NZ, (z + NZ - 2 * i - 2) % NZ, (z + 2 * i + 2) % NZ]
            if wait:
                for j in near:
                    arrive(j)
            work(near)

        last = [(z + NZ // 2 + 1) % NZ, (z + NZ // 2 - 1) % NZ, (z + NZ // 2) % NZ]
        if wait:
            for j in last:
                arrive(j)
        work(last)
        dkv[:, :HD] = dkv[:, :HD] * SCALE

    pair_k.wait_recv()
    pair_v.wait_recv()
    keys(pk, pv, ctx_id(1 - yl, z), True)
    out_kv[...] = dkv[...].astype(BF16)
    kv_copy = rcopy(out_kv, in_kv, psend.at[3], precv.at[3], dev_p)
    kv_copy.start()
    dq_copy.wait_recv()
    gq[:, :HD] = (dqt[:, :TOK] + in_x[...].astype(F32)).T.astype(BF16)
    keys(kall.at[z], vall.at[z], ctx, False)
    kv_copy.wait_recv()
    gq[:, HD:] = (dkv[...] + in_kv[...].astype(F32)).astype(BF16)

    zl, zh = z % 4, z // 4

    def patch_dev(i):
        return (ctx_id(i // 4, zh * 4 + i % 4), f)

    me = yl * 4 + zl
    far_z = [(ctx_id(yl, (z + 4 * i) % NZ), f) for i in range(1, 4)]

    n8 = NX * NYH

    def grad_in(first):
        for s in range(first, first + 4):
            ghid[:, s * ROWS : (s + 1) * ROWS] = nt(gq[...], wall[s]).astype(BF16)
        cols = pl.ds(first * ROWS, 4 * ROWS)
        pltpu.make_async_copy(ghid.at[:, cols], ghid_out.at[:, cols], loc.at[3 + first // 4]).start()

    def block(s):
        return nn(hid_t[s], gq[...])

    def at(xx, yy):
        return xx * NYH + yy

    rsent = []

    def rsend(src, dst, slot, dev):
        copy = rcopy(src, dst, nsend.at[len(rsent)], nrecv.at[slot], dev)
        copy.start()
        rsent.append(copy)

    def rarrived(ref, slot):
        rcopy(ref, ref, nsend.at[0], nrecv.at[slot], dev_s).wait_recv()

    def up(ref):
        return ref[...].astype(F32)

    turns = (0, 2, 1, 3)

    def quarter(q):
        return pl.ds(q * (HALF // 2), HALF // 2)

    order = [
        at(far, yc), at(left, yc), at(right, yc), at(far, yh), at(x, yc), at(right, yh), at(left, yh), at(x, yh)
    ]
    for n, i in enumerate(order):
        sbuf[i] = block(2 * i + 1 - core).astype(BF16)
        rcopy(sbuf.at[i], sbuf_in.at[i], csend.at[n], crecv.at[n], dev_s).start()
    for n, i in enumerate(order):
        mine = block(2 * i + core)
        rcopy(sbuf_in.at[i], sbuf_in.at[i], csend.at[n], crecv.at[n], dev_s).wait_recv()
        term[i] = (mine + up(sbuf_in.at[i])).astype(BF16)
        if n == 0:
            for q in turns:
                rsend(term.at[i, quarter(q)], got.at[0, quarter(q)], q, dev_y)
        elif n < 3:
            to, dev = ((2, dev_l), (1, dev_r))[n - 1]
            for h, rows in enumerate((lo, hi)):
                rsend(term.at[i, rows], got.at[to, rows], 2 + 2 * to + h, dev)
    grad_in(0)
    t_far, t_c, t_r, t_l = at(far, yh), at(x, yc), at(right, yh), at(left, yh)
    for q in turns:
        rows, dev = quarter(q), (dev_r, dev_l)[q // 2]
        rarrived(got.at[0, rows], q)
        relay[0, rows] = (up(term.at[t_far, rows]) + up(got.at[0, rows])).astype(BF16)
        rsend(relay.at[0, rows], gotb.at[rows], 12 + q, dev)
    for h, rows in enumerate((lo, hi)):
        rarrived(got.at[1, rows], 4 + h)
        rarrived(got.at[2, rows], 6 + h)
        relay[1, rows] = (up(term.at[t_c, rows]) + up(got.at[1, rows]) + up(got.at[2, rows])).astype(BF16)
        rsend(relay.at[1, rows], got.at[5, rows], 8 + h, dev_y)
        if h == 0:
            rsend(term.at[t_r, hi], got.at[3, hi], 10, dev_r)
            rsend(term.at[t_l, lo], got.at[4, lo], 11, dev_l)
    for q in turns:
        rows, dev, mine, to = quarter(q), (dev_r, dev_l)[q // 2], (t_r, t_l)[q // 2], 3 + q // 2
        rarrived(gotb.at[rows], 12 + q)
        relay[2, rows] = (up(term.at[mine, rows]) + up(gotb.at[rows])).astype(BF16)
        rsend(relay.at[2, rows], got.at[to, rows], 16 + q, dev)
    for ref, slot in ((got.at[5, lo], 8), (got.at[5, hi], 9), (got.at[3, hi], 10), (got.at[4, lo], 11)):
        rarrived(ref, slot)
    for q in turns:
        rarrived(got.at[3 + q // 2, quarter(q)], 16 + q)
    total[...] = up(term.at[at(x, yh)]) + up(got.at[3]) + up(got.at[4]) + up(got.at[5])
    prt[...] = total[...].astype(BF16).reshape(PATCH, SLICE, QKV)

    for i in range(1, PATCH):
        to = (me + i) % PATCH
        copy = rcopy(prt.at[to], prt_in.at[i], asend.at[i], arecv.at[i], patch_dev(to))
        copy.start()
        rsent.append(copy)
    grad_in(4)
    run = total[pl.ds(pl.multiple_of(me * SLICE, SLICE), SLICE), :]
    for i in range(1, PATCH):
        rcopy(prt_in.at[i], prt_in.at[i], asend.at[i], arecv.at[i], dev_s).wait_recv()
        run += prt_in[i].astype(F32)
    mid[...] = run.astype(BF16)
    for i in range(1, 4):
        copy = rcopy(mid, mid_in.at[i], asend.at[7 + i], arecv.at[7 + i], far_z[i - 1])
        copy.start()
        rsent.append(copy)
    grad_in(8)
    for i in range(1, 4):
        rcopy(mid_in.at[i], mid_in.at[i], asend.at[7 + i], arecv.at[7 + i], dev_s).wait_recv()
    mid_in[0] = mid[...]
    run = jnp.zeros((SLICE, QKV), F32)
    for h in range(4):
        run += mid_in[(zh - h + 4) % 4].astype(F32)
    fin[me] = run.astype(BF16)
    for i in range(1, PATCH):
        to = (me + i) % PATCH
        copy = rcopy(fin.at[me], fin.at[me], asend.at[10 + i], arecv.at[10 + i], patch_dev(to))
        copy.start()
        rsent.append(copy)
    grad_in(12)
    for i in range(1, PATCH):
        src = fin.at[(me + PATCH - i) % PATCH]
        rcopy(src, src, asend.at[10 + i], arecv.at[10 + i], dev_s).wait_recv()
    gw_out[...] = fin[...].reshape(ROWS, QKV).astype(F32)
    for copy in sent + rsent + [do_pair, pair_q, pair_k, pair_v, dq_copy, kv_copy]:
        copy.wait_send()
    for u in range(4):
        ring_end(u)

    @pl.loop(1, NZ)
    def _(d):
        rcopy(stats.at[z], stats.at[z], ssend.at[d], srecv.at[d], dev_p).wait_send()

    @pl.loop(0, n8)
    def _(i):
        rcopy(sbuf.at[i], sbuf_in.at[i], csend.at[i], crecv.at[i], dev_s).wait_send()

    for first in range(0, NX * NYH * NC, 4):
        cols = pl.ds(first * ROWS, 4 * ROWS)
        pltpu.make_async_copy(ghid.at[:, cols], ghid_out.at[:, cols], loc.at[3 + first // 4]).wait()


def step(pages, hidden, w, grad_out):
    n, n8 = NX * NYH * NC, NX * NYH
    hbm = pl.BlockSpec(memory_space=pltpu.HBM)
    vmem = pl.BlockSpec(memory_space=pltpu.VMEM)
    dma = pltpu.SemaphoreType.DMA
    return pl.pallas_call(
        step_kernel,
        out_shape=(
            jax.ShapeDtypeStruct((TOK, D), BF16),
            jax.ShapeDtypeStruct((ROWS, QKV), F32),
        ),
        in_specs=[pl.BlockSpec(memory_space=pltpu.SMEM)] + [hbm] * 3,
        out_specs=(hbm, vmem),
        scratch_shapes=[
            pltpu.VMEM((TOK, D), BF16),
            pltpu.VMEM((n, ROWS, QKV), BF16),
            pltpu.VMEM((TOK, QKV), F32),
            pltpu.VMEM((TOK, QKV), BF16),
            pltpu.VMEM((TOK, HD), BF16),
            pltpu.VMEM((TOK, HD), BF16),
            pltpu.VMEM((NZ, TOK, HD), BF16),
            pltpu.VMEM((NZ, TOK, HD), BF16),
            pltpu.VMEM((NZ, TOK, HD), BF16),
            pltpu.VMEM((NZ, TOK, HD), BF16),
            pltpu.VMEM((TOK, HD), BF16),
            pltpu.VMEM((2 * TOK, HD), BF16),
            pltpu.VMEM((2 * TOK, HD), BF16),
            pltpu.VMEM((1, 2 * TOK), jnp.int32),
            pltpu.VMEM((NZ, 1, TOK), jnp.int32),
            pltpu.VMEM((NZ, TOK, 2 * TOK), F32),
            pltpu.VMEM((NZ, TOK, 2 * TOK), F32),
            pltpu.VMEM((8, 2 * TOK), F32),
            pltpu.VMEM((8, 2 * TOK), F32),
            pltpu.VMEM((NZ, 1, 2 * TOK), F32),
            pltpu.VMEM((HD, 2 * TOK), F32),
            pltpu.VMEM((TOK, 2 * HD), F32),
            pltpu.VMEM((HD, TOK), BF16),
            pltpu.VMEM((HD, TOK), BF16),
            pltpu.VMEM((TOK, 2 * HD), BF16),
            pltpu.VMEM((TOK, 2 * HD), BF16),
            dma((21,)),
            dma((21,)),
            dma((4, 2, NZ // 2)),
            dma((4, 2, NZ // 2 + 1)),
            dma((7,)),
            dma((7,)),
            dma((NZ,)),
            dma((NZ,)),
            dma((7,)),
            pltpu.VMEM((TOK, QKV), BF16),
            pltpu.VMEM((n, ROWS, TOK), BF16),
            pltpu.VMEM((TOK, D), BF16),
            pltpu.VMEM((n8, ROWS, QKV), BF16),
            pltpu.VMEM((n8, ROWS, QKV), BF16),
            pltpu.VMEM((n8, ROWS, QKV), BF16),
            pltpu.VMEM((6, ROWS, QKV), BF16),
            pltpu.VMEM((ROWS, QKV), BF16),
            pltpu.VMEM((3, ROWS, QKV), BF16),
            pltpu.VMEM((ROWS, QKV), F32),
            pltpu.VMEM((PATCH, SLICE, QKV), BF16),
            pltpu.VMEM((PATCH, SLICE, QKV), BF16),
            pltpu.VMEM((SLICE, QKV), BF16),
            pltpu.VMEM((4, SLICE, QKV), BF16),
            pltpu.VMEM((PATCH, SLICE, QKV), BF16),
            dma((n8,)),
            dma((n8,)),
            dma((20,)),
            dma((20,)),
            dma((18,)),
            dma((18,)),
        ],
        compiler_params=pltpu.CompilerParams(
            collective_id=0, has_side_effects=True, vmem_limit_bytes=60 << 20
        ),
        name="step",
    )(pages, hidden, w, grad_out)


def write_kernel(ghid, gw, ghid_out, gw_out, buf, buf_w, sem_in, sem_out):
    rows = TOK // WRITES
    legs = [
        (
            pltpu.make_async_copy(src, via, sem_in.at[i]),
            pltpu.make_async_copy(via, dst, sem_out.at[i]),
        )
        for i, (src, via, dst) in enumerate(
            [(gw, buf_w, gw_out)]
            + [tuple(ref.at[pl.ds(i * rows, rows)] for ref in (ghid, buf, ghid_out)) for i in range(WRITES)]
        )
    ]
    for fetch, _ in legs:
        fetch.start()
    for fetch, store in legs:
        fetch.wait()
        store.start()
    for _, store in legs:
        store.wait()


def write(ghid, gw):
    any_spec = pl.BlockSpec(memory_space=pl.ANY)
    return pl.pallas_call(
        write_kernel,
        out_shape=(jax.ShapeDtypeStruct(ghid.shape, BF16), jax.ShapeDtypeStruct(gw.shape, F32)),
        in_specs=[any_spec] * 2,
        out_specs=(any_spec, any_spec),
        scratch_shapes=[
            pltpu.VMEM(ghid.shape, BF16),
            pltpu.VMEM(gw.shape, F32),
            pltpu.SemaphoreType.DMA((WRITES + 1,)),
            pltpu.SemaphoreType.DMA((WRITES + 1,)),
        ],
        compiler_params=pltpu.CompilerParams(vmem_limit_bytes=60 << 20),
        name="write",
    )(ghid, gw)


def local(hidden_in, page_tokens, grad_attn, w_qkv):
    grad_hidden, grad_w = write(*step(page_tokens, hidden_in[0], w_qkv, grad_attn[0]))
    return grad_hidden[None], grad_w


def solution(mesh):
    in_specs = (P("fsdp", "ctx", None), P("fsdp", None), P("fsdp", "ctx", None), P("fsdp", None))
    out_specs = (P("fsdp", "ctx", None), P("fsdp", None))
    return jax.shard_map(local, mesh=mesh, in_specs=in_specs, out_specs=out_specs, check_vma=False)
```

```python
import functools

import jax
import jax.numpy as jnp
from jax import lax
from jax.experimental import pallas as pl
from jax.experimental.pallas import tpu as pltpu
from jax.sharding import PartitionSpec as P

MESH = pl.DeviceIdType.MESH
F32, BF16 = jnp.float32, jnp.bfloat16
NX, NYH, NC, NYL, NZ = 4, 2, 2, 2, 16
TOK, HD, D = 256, 128, 4096
QKV = 3 * HD
ROWS = D // (NX * NYH * NC)
NEG = -1e30
SCALE = HD ** -0.5
LOG2E = 1.4426950408889634
SCALE2 = SCALE * LOG2E
REACH = 5
WRITES = 8
HALF = TOK // 2
PAGES = 16
LAG = 2
PATCH = 8
SLICE = ROWS // PATCH


def fsdp_id(x, yh, core):
    return (x * NYH + yh) * NC + core


def ctx_id(yl, z):
    return yl * NZ + z


def place():
    ctx, f = lax.axis_index("ctx"), lax.axis_index("fsdp")
    return ctx // NZ, ctx % NZ, f // (NYH * NC), (f // NC) % NYH, f % NC


def rcopy(src, dst, send, recv, dev):
    return pltpu.make_async_remote_copy(
        src_ref=src, dst_ref=dst, send_sem=send, recv_sem=recv, device_id=dev, device_id_type=MESH
    )


def greet(peers):
    barrier = pltpu.get_barrier_semaphore()
    for dev in peers:
        pl.semaphore_signal(barrier, inc=1, device_id=dev, device_id_type=MESH)
    pl.semaphore_wait(barrier, len(peers))


def nt(a, b):
    return lax.dot_general(a, b, (((1,), (1,)), ((), ())), preferred_element_type=F32)


def tn(a, b):
    return lax.dot_general(a, b, (((0,), (0,)), ((), ())), preferred_element_type=F32)


def nn(a, b):
    return jnp.dot(a, b, preferred_element_type=F32)


def neighbours():
    yl, z, x, yh, core = place()
    ctx, f = ctx_id(yl, z), fsdp_id(x, yh, core)
    left, right = (x + NX - 1) % NX, (x + 1) % NX
    dev_l, dev_r = (ctx, fsdp_id(left, yh, core)), (ctx, fsdp_id(right, yh, core))
    dev_y = (ctx_id(1 - yl, z), fsdp_id(x, 1 - yh, core))
    dev_s = (ctx, fsdp_id(x, yh, 1 - core))
    return dev_l, dev_r, dev_y, dev_s


def step_kernel(
    pages, hid_hbm, w_hbm, do_hbm, ghid_out, gw_out,
    hid, wall, acc, proj, pk, pv, kall, vall, qall, doall, pdo, q2, do2, lim_q, lim_col, s_keep, dp_keep, mlu, mlu_in,
    stats, dqt, dkv, out_x, in_x, out_kv, in_kv, wsend, wrecv, zsend, zrecv, psend, precv, ssend, srecv, loc,
    gq, hid_t, ghid, term, sbuf, sbuf_in, got, gotb, relay, total, prt, prt_in, mid, mid_in, fin, csend, crecv, nsend, nrecv, asend, arecv,
):
    yl, z, x, yh, core = place()
    ctx, f = ctx_id(yl, z), fsdp_id(x, yh, core)
    left, right, far = (x + NX - 1) % NX, (x + 1) % NX, (x + 2) % NX
    dev_l, dev_r, dev_y, dev_s = neighbours()
    dev_p = (ctx_id(1 - yl, z), f)

    def at_z(d):
        return (ctx_id(yl, (z + d) % NZ), f)

    dev_zl, dev_zr = at_z(NZ - 1), at_z(1)
    greet([dev_l, dev_r, dev_y, dev_s, dev_p, dev_zl, dev_zr])

    sent = []

    def send(src, dst, slot, dev):
        copy = rcopy(src, dst, wsend.at[len(sent)], wrecv.at[slot], dev)
        copy.start()
        sent.append(copy)

    def arrived(ref, slot):
        rcopy(ref, ref, wsend.at[0], wrecv.at[slot], dev_s).wait_recv()

    rings = ((kall, 8, 7), (vall, 7, 8), (qall, 8, 7), (doall, 7, 8))

    def ring_start(u, src):
        buf = rings[u][0]
        rcopy(src, buf.at[z], zsend.at[u, 0, 0], zrecv.at[u, 0, 1], dev_zr).start()
        rcopy(src, buf.at[z], zsend.at[u, 1, 0], zrecv.at[u, 1, 1], dev_zl).start()

    def serve(u, d):
        buf, reach_r, reach_l = rings[u]
        for side, reach, dev, j in (
            (0, reach_r, dev_zr, (z + NZ - d) % NZ), (1, reach_l, dev_zl, (z + d) % NZ)
        ):
            @pl.when(d <= reach)
            def _():
                rcopy(buf.at[j], buf.at[j], zsend.at[u, side, 0], zrecv.at[u, side, d], dev).wait_recv()

            @pl.when(d < reach)
            def _():
                rcopy(buf.at[j], buf.at[j], zsend.at[u, side, d], zrecv.at[u, side, d + 1], dev).start()

    def ring_end(u):
        buf, reach_r, reach_l = rings[u]

        @pl.loop(0, NZ // 2)
        def _(d):
            for side, reach, dev in ((0, reach_r, dev_zr), (1, reach_l, dev_zl)):
                @pl.when(d < reach)
                def _():
                    rcopy(buf.at[z], buf.at[z], zsend.at[u, side, d], zrecv.at[u, side, 1], dev).wait_send()

    lo, hi = pl.ds(0, HALF), pl.ds(HALF, HALF)
    for slot, rows, dev in ((1, lo, dev_r), (2, hi, dev_l), (19, hi, dev_r), (20, lo, dev_l)):
        send(w_hbm.at[rows], wall.at[f, rows], slot, dev)
    send(w_hbm, wall.at[f], 0, dev_y)
    send(w_hbm, wall.at[f], 9, dev_s)
    ring_start(3, do_hbm)
    do_pair = rcopy(do_hbm, pdo, psend.at[4], precv.at[4], dev_p)
    do_pair.start()
    hid_copy = pltpu.make_async_copy(hid_hbm, hid, loc.at[0])
    own_copy = pltpu.make_async_copy(w_hbm, wall.at[f], loc.at[1])
    do_copy = pltpu.make_async_copy(do_hbm, doall.at[z], loc.at[2])
    own_copy.start()
    do_copy.start()
    hid_copy.start()

    ends = []
    end = 0
    for page in range(PAGES):
        end = end + pages[0, page]
        ends.append(end)

    def limits(pos):
        out = jnp.full(pos.shape, NYL * NZ * TOK, jnp.int32)
        for stop in ends:
            out = jnp.minimum(out, jnp.where(pos < stop, stop, NYL * NZ * TOK))
        return out

    lane = lax.broadcasted_iota(jnp.int32, (1, TOK), 1)
    lim_q[:, :TOK] = limits(ctx * TOK + lane)
    lim_q[:, TOK:] = limits(ctx_id(1 - yl, z) * TOK + lane)

    @pl.loop(0, NZ)
    def _(j):
        lim_col[j] = limits(ctx_id(yl, j) * TOK + lane)

    mlu[0:1] = jnp.full((1, 2 * TOK), NEG, F32)
    mlu[1:8] = jnp.zeros((7, 2 * TOK), F32)

    def own(xx, yy):
        return fsdp_id(xx, yy, core)

    def sib(xx, yy):
        return fsdp_id(xx, yy, 1 - core)

    def project(shards):
        out = None
        for s in shards:
            term = nn(hid[:, pl.ds(pl.multiple_of(s * ROWS, ROWS), ROWS)], wall[s])
            out = term if out is None else out + term
        return out

    yc = 1 - yh
    serve(3, 1)
    ol, orr = wall.at[own(left, yh)], wall.at[own(right, yh)]
    on = wall.at[own(left, yh), lo]
    arrived(on, 1)
    send(on, on, 5, dev_r)
    on = wall.at[own(right, yh), hi]
    arrived(on, 2)
    send(on, on, 6, dev_l)
    c = wall.at[own(x, yc)]
    arrived(c, 0)
    send(c, c, 3, dev_r)
    send(c, c, 4, dev_l)
    arrived(wall.at[own(left, yh), hi], 19)
    send(ol, ol, 11, dev_s)
    arrived(wall.at[own(right, yh), lo], 20)
    send(orr, orr, 12, dev_s)
    send(c, c, 10, dev_s)
    serve(3, 2)
    hid_copy.wait()
    own_copy.wait()
    do_copy.wait()
    acc[...] = project([f, own(x, yc), own(left, yh), own(right, yh)])
    fa, fb = wall.at[own(far, yh), lo], wall.at[own(far, yh), hi]
    arrived(fa, 5)
    send(fa, fa, 7, dev_y)
    send(fa, fa, 15, dev_s)
    arrived(fb, 6)
    send(fb, fb, 8, dev_y)
    send(fb, fb, 16, dev_s)
    serve(3, 3)
    for slot, ref in (
        (9, wall.at[sib(x, yh)]), (10, wall.at[sib(x, yc)]), (11, wall.at[sib(left, yh)]),
        (12, wall.at[sib(right, yh)]),
    ):
        arrived(ref, slot)
    acc[...] += project([sib(x, yh), sib(x, yc), sib(left, yh), sib(right, yh)])
    serve(3, 4)
    cl, cr = wall.at[own(left, yc)], wall.at[own(right, yc)]
    arrived(cl, 3)
    send(cl, cl, 13, dev_s)
    arrived(cr, 4)
    send(cr, cr, 14, dev_s)
    acc[...] += project([own(left, yc), own(right, yc), own(far, yh)])
    ca, cb = wall.at[own(far, yc), lo], wall.at[own(far, yc), hi]
    arrived(ca, 7)
    send(ca, ca, 17, dev_s)
    arrived(cb, 8)
    send(cb, cb, 18, dev_s)
    for slot, ref in (
        (13, wall.at[sib(left, yc)]), (14, wall.at[sib(right, yc)]), (15, wall.at[sib(far, yh), lo]),
        (16, wall.at[sib(far, yh), hi]), (17, wall.at[sib(far, yc), lo]), (18, wall.at[sib(far, yc), hi]),
    ):
        arrived(ref, slot)
    acc[...] += project([own(far, yc), sib(left, yc), sib(right, yc), sib(far, yh), sib(far, yc)])
    proj[...] = acc[...].astype(BF16)
    kall[z] = proj[:, HD : 2 * HD]
    vall[z] = proj[:, 2 * HD :]
    ring_start(0, kall.at[z])
    ring_start(1, vall.at[z])
    qall[z] = proj[:, :HD]
    pair_q = rcopy(qall.at[z], q2.at[pl.ds(TOK, TOK)], psend.at[0], precv.at[0], dev_p)
    pair_q.start()
    pair_k = rcopy(kall.at[z], pk, psend.at[5], precv.at[5], dev_p)
    pair_k.start()
    pair_v = rcopy(vall.at[z], pv, psend.at[6], precv.at[6], dev_p)
    pair_v.start()
    q2[:TOK] = proj[:, :HD]
    do2[:TOK] = doall[z]
    serve(3, 5)

    key_row = lax.broadcasted_iota(jnp.int32, (TOK, 1), 0)
    last_q = ctx_id(1, z)

    def score(j, also):
        @pl.when(also & (ctx_id(yl, j) <= last_q + REACH))
        def _():
            s = nt(kall[j], q2[...]) * SCALE2
            dp = nt(vall[j], do2[...])
            s = jnp.where(ctx_id(yl, j) * TOK + key_row < lim_q[...], s, NEG)
            s_keep[j] = s
            dp_keep[j] = dp
            m = mlu[0:1]
            m_new = jnp.maximum(m, jnp.max(s, axis=0, keepdims=True))
            p = jnp.exp2(s - m_new)
            a = jnp.exp2(m - m_new)
            mlu[0:1] = m_new
            mlu[1:2] = mlu[1:2] * a + jnp.sum(p, axis=0, keepdims=True)
            mlu[2:3] = mlu[2:3] * a + jnp.sum(p * dp, axis=0, keepdims=True)

    @pl.loop(1, NZ // 2 + 1)
    def _(k):
        serve(0, k)
        serve(1, k)

        @pl.when(k < 4)
        def _():
            serve(3, k + 5)

        @pl.when(k == 1)
        def _():
            do_pair.wait_recv()
            do2[TOK:] = pdo[...]
            pair_q.wait_recv()

        @pl.when(k == LAG)
        def _():
            ring_start(2, qall.at[z])

        @pl.when(k > LAG)
        def _():
            serve(2, k - LAG)

        @pl.loop(0, 2)
        def _(side):
            score((z + NZ - (k - 1) + 2 * (k - 1) * side) % NZ, (side == 0) | (k > 1))
            n = 2 * (k - 1) + side
            hid_t[n] = hid[:, pl.ds(pl.multiple_of(n * ROWS, ROWS), ROWS)].T

    score((z + NZ // 2) % NZ, True)

    trade = rcopy(mlu, mlu_in, psend.at[1], precv.at[1], dev_p)
    trade.start()
    serve(2, NZ // 2 - LAG + 1)
    trade.wait_recv()

    def merge(mine, theirs):
        m1, m2 = mlu[0:1, mine], mlu_in[0:1, theirs]
        m = jnp.maximum(m1, m2)
        a1, a2 = jnp.exp2(m1 - m), jnp.exp2(m2 - m)
        l = mlu[1:2, mine] * a1 + mlu_in[1:2, theirs] * a2
        u = mlu[2:3, mine] * a1 + mlu_in[2:3, theirs] * a2
        return m + jnp.log(l) * LOG2E, u / l

    own_q, par_q = slice(0, TOK), slice(TOK, 2 * TOK)
    lse_own, dot_own = merge(own_q, par_q)
    lse_par, dot_par = merge(par_q, own_q)
    stats[z, :, :TOK] = lse_own
    stats[z, :, TOK:] = dot_own

    @pl.loop(1, NZ)
    def _(i):
        rcopy(stats.at[z], stats.at[z], ssend.at[i], srecv.at[i], at_z(i)).start()

    trade.wait_send()
    mlu[0:1] = jnp.concatenate([lse_own, lse_par], axis=1)
    mlu[1:2] = jnp.concatenate([dot_own, dot_par], axis=1)
    dqt[...] = jnp.zeros((HD, 2 * TOK), F32)

    @pl.loop(0, NZ // 4)
    def _(i):
        @pl.when(ctx_id(yl, 4 * i) <= last_q + REACH)
        def _():
            for n in range(1, 4):
                @pl.when(ctx_id(yl, 4 * i + n) > last_q + REACH)
                def _():
                    s_keep[4 * i + n] = jnp.full((TOK, 2 * TOK), NEG, F32)
                    dp_keep[4 * i + n] = jnp.zeros((TOK, 2 * TOK), F32)

            out = []
            for n in range(4):
                j = 4 * i + n
                p = jnp.exp2(s_keep[j] - mlu[0:1])
                ds = (p * (dp_keep[j] - mlu[1:2])).astype(BF16)
                out.append(tn(kall[j], ds))
            dqt[...] += (out[0] + out[1]) + (out[2] + out[3])

        @pl.when((i == 1) & (LAG > 1))
        def _():
            serve(2, NZ // 2)

    dqt[...] = dqt[...] * SCALE
    out_x[...] = dqt[:, TOK:].astype(BF16)
    dq_copy = rcopy(out_x, in_x, psend.at[2], precv.at[2], dev_p)
    dq_copy.start()

    def keys(k_src, v_src, k_block, wait):
        dkv[...] = jnp.zeros((TOK, 2 * HD), F32)

        def arrive(j):
            n = (z + NZ - j) % NZ
            rcopy(stats.at[j], stats.at[j], ssend.at[n], srecv.at[n], dev_p).wait_recv()

        def work(blocks):
            seen = k_block <= ctx_id(yl, blocks[0]) + REACH
            for j in blocks[1:]:
                seen = seen | (k_block <= ctx_id(yl, j) + REACH)

            edge = k_block >= ctx_id(yl, blocks[0])
            for j in blocks[1:]:
                edge = edge | (k_block >= ctx_id(yl, j))

            def tiles(masked):
                dk, dv = [], []
                for j in blocks:
                    s = nt(k_src[...], qall[j]) * SCALE2
                    dp = nt(v_src[...], doall[j])
                    if masked:
                        s = jnp.where(k_block * TOK + key_row < lim_col[j], s, NEG)
                    p = jnp.exp2(s - stats[j, :, :TOK])
                    ds = (p * (dp - stats[j, :, TOK:])).astype(BF16)
                    dk.append(nn(ds, qall[j]))
                    dv.append(nn(p.astype(BF16), doall[j]))
                dkv[:, :HD] += sum(dk[1:], dk[0])
                dkv[:, HD:] += sum(dv[1:], dv[0])

            pl.when(seen & edge)(lambda: tiles(True))
            pl.when(seen & jnp.logical_not(edge))(lambda: tiles(False))

        work([z])

        @pl.loop(0, NZ // 4 - 1)
        def _(i):
            near = [(z + NZ - 2 * i - 1) % NZ, (z + 2 * i + 1) % NZ, (z + NZ - 2 * i - 2) % NZ, (z + 2 * i + 2) % NZ]
            if wait:
                for j in near:
                    arrive(j)
            work(near)

        last = [(z + NZ // 2 + 1) % NZ, (z + NZ // 2 - 1) % NZ, (z + NZ // 2) % NZ]
        if wait:
            for j in last:
                arrive(j)
        work(last)
        dkv[:, :HD] = dkv[:, :HD] * SCALE

    pair_k.wait_recv()
    pair_v.wait_recv()
    keys(pk, pv, ctx_id(1 - yl, z), True)
    out_kv[...] = dkv[...].astype(BF16)
    kv_copy = rcopy(out_kv, in_kv, psend.at[3], precv.at[3], dev_p)
    kv_copy.start()
    dq_copy.wait_recv()
    gq[:, :HD] = (dqt[:, :TOK] + in_x[...].astype(F32)).T.astype(BF16)
    keys(kall.at[z], vall.at[z], ctx, False)
    kv_copy.wait_recv()
    gq[:, HD:] = (dkv[...] + in_kv[...].astype(F32)).astype(BF16)

    zl, zh = z % 4, z // 4

    def patch_dev(i):
        return (ctx_id(i // 4, zh * 4 + i % 4), f)

    me = yl * 4 + zl
    far_z = [(ctx_id(yl, (z + 4 * i) % NZ), f) for i in range(1, 4)]

    n8 = NX * NYH

    def grad_in(first):
        for s in range(first, first + 4):
            ghid[:, s * ROWS : (s + 1) * ROWS] = nt(gq[...], wall[s]).astype(BF16)
        cols = pl.ds(first * ROWS, 4 * ROWS)
        pltpu.make_async_copy(ghid.at[:, cols], ghid_out.at[:, cols], loc.at[3 + first // 4]).start()

    def block(s):
        return nn(hid_t[s], gq[...])

    def at(xx, yy):
        return xx * NYH + yy

    rsent = []

    def rsend(src, dst, slot, dev):
        copy = rcopy(src, dst, nsend.at[len(rsent)], nrecv.at[slot], dev)
        copy.start()
        rsent.append(copy)

    def rarrived(ref, slot):
        rcopy(ref, ref, nsend.at[0], nrecv.at[slot], dev_s).wait_recv()

    def up(ref):
        return ref[...].astype(F32)

    turns = (0, 2, 1, 3)

    def quarter(q):
        return pl.ds(q * (HALF // 2), HALF // 2)

    order = [
        at(far, yc), at(left, yc), at(right, yc), at(far, yh), at(x, yc), at(right, yh), at(left, yh), at(x, yh)
    ]
    for n, i in enumerate(order):
        sbuf[i] = block(2 * i + 1 - core).astype(BF16)
        rcopy(sbuf.at[i], sbuf_in.at[i], csend.at[n], crecv.at[n], dev_s).start()
    for n, i in enumerate(order):
        mine = block(2 * i + core)
        rcopy(sbuf_in.at[i], sbuf_in.at[i], csend.at[n], crecv.at[n], dev_s).wait_recv()
        term[i] = (mine + up(sbuf_in.at[i])).astype(BF16)
        if n == 0:
            for q in turns:
                rsend(term.at[i, quarter(q)], got.at[0, quarter(q)], q, dev_y)
        elif n < 3:
            to, dev = ((2, dev_l), (1, dev_r))[n - 1]
            for h, rows in enumerate((lo, hi)):
                rsend(term.at[i, rows], got.at[to, rows], 2 + 2 * to + h, dev)
    grad_in(0)
    t_far, t_c, t_r, t_l = at(far, yh), at(x, yc), at(right, yh), at(left, yh)
    for q in turns:
        rows, dev = quarter(q), (dev_r, dev_l)[q // 2]
        rarrived(got.at[0, rows], q)
        relay[0, rows] = (up(term.at[t_far, rows]) + up(got.at[0, rows])).astype(BF16)
        rsend(relay.at[0, rows], gotb.at[rows], 12 + q, dev)
    for h, rows in enumerate((lo, hi)):
        rarrived(got.at[1, rows], 4 + h)
        rarrived(got.at[2, rows], 6 + h)
        relay[1, rows] = (up(term.at[t_c, rows]) + up(got.at[1, rows]) + up(got.at[2, rows])).astype(BF16)
        rsend(relay.at[1, rows], got.at[5, rows], 8 + h, dev_y)
        if h == 0:
            rsend(term.at[t_r, hi], got.at[3, hi], 10, dev_r)
            rsend(term.at[t_l, lo], got.at[4, lo], 11, dev_l)
    for q in turns:
        rows, dev, mine, to = quarter(q), (dev_r, dev_l)[q // 2], (t_r, t_l)[q // 2], 3 + q // 2
        rarrived(gotb.at[rows], 12 + q)
        relay[2, rows] = (up(term.at[mine, rows]) + up(gotb.at[rows])).astype(BF16)
        rsend(relay.at[2, rows], got.at[to, rows], 16 + q, dev)
    for ref, slot in ((got.at[5, lo], 8), (got.at[5, hi], 9), (got.at[3, hi], 10), (got.at[4, lo], 11)):
        rarrived(ref, slot)
    for q in turns:
        rarrived(got.at[3 + q // 2, quarter(q)], 16 + q)
    total[...] = up(term.at[at(x, yh)]) + up(got.at[3]) + up(got.at[4]) + up(got.at[5])
    prt[...] = total[...].astype(BF16).reshape(PATCH, SLICE, QKV)

    for i in range(1, PATCH):
        to = (me + i) % PATCH
        copy = rcopy(prt.at[to], prt_in.at[i], asend.at[i], arecv.at[i], patch_dev(to))
        copy.start()
        rsent.append(copy)
    grad_in(4)
    run = total[pl.ds(pl.multiple_of(me * SLICE, SLICE), SLICE), :]
    for i in range(1, PATCH):
        rcopy(prt_in.at[i], prt_in.at[i], asend.at[i], arecv.at[i], dev_s).wait_recv()
        run += prt_in[i].astype(F32)
    mid[...] = run.astype(BF16)
    for i in range(1, 4):
        copy = rcopy(mid, mid_in.at[i], asend.at[7 + i], arecv.at[7 + i], far_z[i - 1])
        copy.start()
        rsent.append(copy)
    grad_in(8)
    for i in range(1, 4):
        rcopy(mid_in.at[i], mid_in.at[i], asend.at[7 + i], arecv.at[7 + i], dev_s).wait_recv()
    mid_in[0] = mid[...]
    run = jnp.zeros((SLICE, QKV), F32)
    for h in range(4):
        run += mid_in[(zh - h + 4) % 4].astype(F32)
    fin[me] = run.astype(BF16)
    for i in range(1, PATCH):
        to = (me + i) % PATCH
        copy = rcopy(fin.at[me], fin.at[me], asend.at[10 + i], arecv.at[10 + i], patch_dev(to))
        copy.start()
        rsent.append(copy)
    grad_in(12)
    for i in range(1, PATCH):
        src = fin.at[(me + PATCH - i) % PATCH]
        rcopy(src, src, asend.at[10 + i], arecv.at[10 + i], dev_s).wait_recv()
    gw_out[...] = fin[...].reshape(ROWS, QKV).astype(F32)
    for copy in sent + rsent + [do_pair, pair_q, pair_k, pair_v, dq_copy, kv_copy]:
        copy.wait_send()
    for u in range(4):
        ring_end(u)

    @pl.loop(1, NZ)
    def _(d):
        rcopy(stats.at[z], stats.at[z], ssend.at[d], srecv.at[d], dev_p).wait_send()

    @pl.loop(0, n8)
    def _(i):
        rcopy(sbuf.at[i], sbuf_in.at[i], csend.at[i], crecv.at[i], dev_s).wait_send()

    for first in range(0, NX * NYH * NC, 4):
        cols = pl.ds(first * ROWS, 4 * ROWS)
        pltpu.make_async_copy(ghid.at[:, cols], ghid_out.at[:, cols], loc.at[3 + first // 4]).wait()


def step(pages, hidden, w, grad_out):
    n, n8 = NX * NYH * NC, NX * NYH
    hbm = pl.BlockSpec(memory_space=pltpu.HBM)
    vmem = pl.BlockSpec(memory_space=pltpu.VMEM)
    dma = pltpu.SemaphoreType.DMA
    return pl.pallas_call(
        step_kernel,
        out_shape=(
            jax.ShapeDtypeStruct((TOK, D), BF16),
            jax.ShapeDtypeStruct((ROWS, QKV), F32),
        ),
        in_specs=[pl.BlockSpec(memory_space=pltpu.SMEM)] + [hbm] * 3,
        out_specs=(hbm, vmem),
        scratch_shapes=[
            pltpu.VMEM((TOK, D), BF16),
            pltpu.VMEM((n, ROWS, QKV), BF16),
            pltpu.VMEM((TOK, QKV), F32),
            pltpu.VMEM((TOK, QKV), BF16),
            pltpu.VMEM((TOK, HD), BF16),
            pltpu.VMEM((TOK, HD), BF16),
            pltpu.VMEM((NZ, TOK, HD), BF16),
            pltpu.VMEM((NZ, TOK, HD), BF16),
            pltpu.VMEM((NZ, TOK, HD), BF16),
            pltpu.VMEM((NZ, TOK, HD), BF16),
            pltpu.VMEM((TOK, HD), BF16),
            pltpu.VMEM((2 * TOK, HD), BF16),
            pltpu.VMEM((2 * TOK, HD), BF16),
            pltpu.VMEM((1, 2 * TOK), jnp.int32),
            pltpu.VMEM((NZ, 1, TOK), jnp.int32),
            pltpu.VMEM((NZ, TOK, 2 * TOK), F32),
            pltpu.VMEM((NZ, TOK, 2 * TOK), F32),
            pltpu.VMEM((8, 2 * TOK), F32),
            pltpu.VMEM((8, 2 * TOK), F32),
            pltpu.VMEM((NZ, 1, 2 * TOK), F32),
            pltpu.VMEM((HD, 2 * TOK), F32),
            pltpu.VMEM((TOK, 2 * HD), F32),
            pltpu.VMEM((HD, TOK), BF16),
            pltpu.VMEM((HD, TOK), BF16),
            pltpu.VMEM((TOK, 2 * HD), BF16),
            pltpu.VMEM((TOK, 2 * HD), BF16),
            dma((21,)),
            dma((21,)),
            dma((4, 2, NZ // 2)),
            dma((4, 2, NZ // 2 + 1)),
            dma((7,)),
            dma((7,)),
            dma((NZ,)),
            dma((NZ,)),
            dma((7,)),
            pltpu.VMEM((TOK, QKV), BF16),
            pltpu.VMEM((n, ROWS, TOK), BF16),
            pltpu.VMEM((TOK, D), BF16),
            pltpu.VMEM((n8, ROWS, QKV), BF16),
            pltpu.VMEM((n8, ROWS, QKV), BF16),
            pltpu.VMEM((n8, ROWS, QKV), BF16),
            pltpu.VMEM((6, ROWS, QKV), BF16),
            pltpu.VMEM((ROWS, QKV), BF16),
            pltpu.VMEM((3, ROWS, QKV), BF16),
            pltpu.VMEM((ROWS, QKV), F32),
            pltpu.VMEM((PATCH, SLICE, QKV), BF16),
            pltpu.VMEM((PATCH, SLICE, QKV), BF16),
            pltpu.VMEM((SLICE, QKV), BF16),
            pltpu.VMEM((4, SLICE, QKV), BF16),
            pltpu.VMEM((PATCH, SLICE, QKV), BF16),
            dma((n8,)),
            dma((n8,)),
            dma((20,)),
            dma((20,)),
            dma((18,)),
            dma((18,)),
        ],
        compiler_params=pltpu.CompilerParams(
            collective_id=0, has_side_effects=True, vmem_limit_bytes=60 << 20
        ),
        name="step",
    )(pages, hidden, w, grad_out)


def write_kernel(ghid, gw, ghid_out, gw_out, buf, buf_w, sem_in, sem_out):
    rows = TOK // WRITES
    legs = [
        (
            pltpu.make_async_copy(src, via, sem_in.at[i]),
            pltpu.make_async_copy(via, dst, sem_out.at[i]),
        )
        for i, (src, via, dst) in enumerate(
            [(gw, buf_w, gw_out)]
            + [tuple(ref.at[pl.ds(i * rows, rows)] for ref in (ghid, buf, ghid_out)) for i in range(WRITES)]
        )
    ]
    for fetch, _ in legs:
        fetch.start()
    for fetch, store in legs:
        fetch.wait()
        store.start()
    for _, store in legs:
        store.wait()


def write(ghid, gw):
    any_spec = pl.BlockSpec(memory_space=pl.ANY)
    return pl.pallas_call(
        write_kernel,
        out_shape=(jax.ShapeDtypeStruct(ghid.shape, BF16), jax.ShapeDtypeStruct(gw.shape, F32)),
        in_specs=[any_spec] * 2,
        out_specs=(any_spec, any_spec),
        scratch_shapes=[
            pltpu.VMEM(ghid.shape, BF16),
            pltpu.VMEM(gw.shape, F32),
            pltpu.SemaphoreType.DMA((WRITES + 1,)),
            pltpu.SemaphoreType.DMA((WRITES + 1,)),
        ],
        compiler_params=pltpu.CompilerParams(vmem_limit_bytes=60 << 20),
        name="write",
    )(ghid, gw)


def local(hidden_in, page_tokens, grad_attn, w_qkv):
    grad_hidden, grad_w = write(*step(page_tokens, hidden_in[0], w_qkv, grad_attn[0]))
    return grad_hidden[None], grad_w


def solution(mesh):
    in_specs = (P("fsdp", "ctx", None), P("fsdp", None), P("fsdp", "ctx", None), P("fsdp", None))
    out_specs = (P("fsdp", "ctx", None), P("fsdp", None))
    return jax.shard_map(local, mesh=mesh, in_specs=in_specs, out_specs=out_specs, check_vma=False)
```
